512 devices in a mesh: dp: 64 (over x, z, y_lo), tp: 8 (over y_hi, core).
Axes of the slice: x: 4, y: 8 (y_hi: 4, y_lo: 2; y = y_hi * 2 + y_lo), z: 8, core: 2. Of those that a mesh axis runs over, the one named last changes fastest.
Arguments:
- stash_values: bfloat16 [65536, 8192], P(('dp', 'tp')), may hold values from -127 to 127
- stash_scales: bfloat16 [65536, 64], P(('dp', 'tp')), may hold values from 0.001 to 0.13
- value_grad: bfloat16 [65536, 1024], P('dp', 'tp'), may hold values from -19 to 19
Outputs:
- clipped_grad: float32 [8192, 1024], P('dp', 'tp')
The draws below stay inside these ranges and needn't reach their ends.
All inputs are finite; a program needn't handle non-finite values.
Results may differ from the reference program's by a relative error of at most 0.0019.
Values may be sent and summed in bfloat16 or wider, within the bound.
A program may use at most 64 MiB of HBM per device.

```python
import math
import jax
import jax.numpy as jnp
from jax import lax

D = 8192
HD = 128
QB = 128
TOK_DEV = 128
KV_HEADS = 8
TOKENS = 65536
N_DP = 64
N_TP = 8


def draw_stash_values(key, part):
    offset_top = min(17, 120 // math.isqrt(math.isqrt(TOKENS)))
    offset_low = 3 * offset_top // 4
    magnitude = jax.random.randint(jax.random.fold_in(key, 18), (D,), offset_low, offset_top + 1)
    sign_draw = 2 * jax.random.randint(jax.random.fold_in(key, 19), (D,), 0, 2) - 1
    noise = jax.random.randint(jax.random.fold_in(key, 17), (TOKENS, D), -110, 111)
    whole = noise + (sign_draw * magnitude)[None, :]
    return whole.astype(jnp.float32).astype(jnp.bfloat16)


def spread_levels(key, count, spread):
    order = jax.random.permutation(jax.random.fold_in(key, 1), count).astype(jnp.float32)
    jitter = jax.random.uniform(jax.random.fold_in(key, 2), (count,), jnp.float32)
    return jnp.exp(spread * (order + jitter) / count - 0.5 * spread)


def draw_stash_scales(key, part):
    blocks = D // QB
    spread = jnp.log(jnp.float32(10.0))
    logs = jax.random.uniform(jax.random.fold_in(key, 34), (TOKENS, blocks), jnp.float32, jnp.log(0.004), jnp.log(0.04))
    base = jnp.exp(logs)
    levels = spread_levels(jax.random.fold_in(key, 31), blocks, spread)
    return (base * levels[None, :]).astype(jnp.bfloat16)


def draw_value_grad(key, part):
    heads = KV_HEADS
    spread = jnp.log(jnp.float32(10.0))
    strength = jnp.float32(1.6)
    noise = jax.random.truncated_normal(jax.random.fold_in(key, 44), -5.4, 5.4, (TOKENS, heads * HD), jnp.float32)
    column_signs = (2 * jax.random.randint(jax.random.fold_in(key, 46), (heads * HD,), 0, 2) - 1).astype(jnp.float32)
    shift = strength * jnp.float32(TOKENS) ** (-0.25) * column_signs
    levels = spread_levels(jax.random.fold_in(key, 41), heads, spread)
    column_levels = jnp.repeat(levels, HD)
    return ((noise + shift[None, :]) * column_levels[None, :]).astype(jnp.bfloat16)


def setup_inputs(seed: int = 0) -> dict:
    streams_of = jax.random.split(jax.random.key(seed), 4)
    return {
        "stash_values": draw_stash_values(jax.random.fold_in(streams_of[3], 71), 0),
        "stash_scales": draw_stash_scales(jax.random.fold_in(streams_of[3], 71), 0),
        "value_grad": draw_value_grad(jax.random.fold_in(streams_of[3], 71), 0),
    }


def reference(stash_values, stash_scales, value_grad):
    width = stash_values.shape[1]
    group = TOK_DEV * N_TP
    columns = value_grad.shape[1]

    def one_group(total, index):
        start = (index * group).astype(jnp.int32)
        values = lax.dynamic_slice_in_dim(stash_values, start, group, 0)
        scales = lax.dynamic_slice_in_dim(stash_scales, start, group, 0)
        grads = lax.dynamic_slice_in_dim(value_grad, start, group, 0)
        blocks = values.astype(jnp.float32).reshape(group, width // QB, QB) * scales.astype(jnp.float32)[:, :, None]
        dequantized = blocks.reshape(group, width).astype(jnp.bfloat16)
        term = jnp.dot(dequantized.astype(jnp.float32).T, grads.astype(jnp.float32), precision=lax.Precision.HIGHEST)
        return (total + term, None)
    start_total = jnp.zeros((width, columns), jnp.float32)
    weight_sum, unused = lax.scan(one_group, start_total, jnp.arange(N_DP, dtype=jnp.int32))
    grad_norm = jnp.sqrt(jnp.sum(weight_sum * weight_sum))
    limit = jnp.sqrt(jnp.float32(width * columns))
    return weight_sum * jnp.minimum(jnp.float32(1.0), limit / grad_norm)
```

```python
import jax
import jax.numpy as jnp
from jax import lax
from jax.experimental import pallas as pl
from jax.experimental.pallas import tpu as pltpu
from jax.sharding import Mesh
from jax.sharding import PartitionSpec as P

MESH = pl.DeviceIdType.MESH
NX, NZ, NH, NL, NC = 4, 8, 4, 2, 2
AXES = ("x", "z", "yl", "yh", "c")
HD = 128
TOK = 128
RX = 80
RZ = HD - RX
PHASES = NH
STAGES = 7
OFFSET = 2
NEWEST_FIRST = False
BF = jnp.bfloat16
F32 = jnp.float32


def mod(value, n):
    return lax.rem(value + 4 * n, n)


def kernel(
    x_hbm, s_ref, g_hbm, out_ref, ss_ref,
    xv, xd, xs, gb, gt, wx, wz,
    rxl, rxs, rzl, rzs, vz, vb, uz, ub,
    r2zl, r2zs, r2xl, r2xs, ty, ry, nsrc, n1, n2, n3,
    ld_sem, g_ss, g_rs, xo_ss, xo_rs, xp_ss, xp_rs, xf_ss, xf_rs,
    xl_ss, xl_rs, xq_ss, xq_rs, zl_ss, zl_rs, zs_ss, zs_rs,
    z2l_ss, z2l_rs, z2s_ss, z2s_rs, x2l_ss, x2l_rs, x2s_ss, x2s_rs,
    y_ss, y_rs, n1_ss, n1_rs, n2_ss, n2_rs, n3_ss, n3_rs,
):
    x, z, yl, yh, c = (lax.axis_index(name) for name in AXES)
    quarter = NZ * 2 * HD

    def push(src, dst, ss, rs, dev):
        pltpu.make_async_remote_copy(
            src_ref=src, dst_ref=dst, send_sem=ss, recv_sem=rs, device_id=dev, device_id_type=MESH
        ).start()

    def arrived(dst, rs):
        pltpu.make_async_remote_copy(
            src_ref=dst, dst_ref=dst, send_sem=rs, recv_sem=rs, device_id={"c": 1 - c}, device_id_type=MESH
        ).wait_recv()

    def sent(src, ss):
        pltpu.make_async_remote_copy(
            src_ref=src, dst_ref=src, send_sem=ss, recv_sem=ss, device_id={"c": 1 - c}, device_id_type=MESH
        ).wait_send()

    def order_x(i):
        return mod(x + jnp.where(i == 0, 2, jnp.where(i == 1, 1, jnp.where(i == 2, 3, 0))), NX)

    def load(i):
        xq = order_x(i)
        cols = pl.ds(pl.multiple_of(xq * quarter, quarter), quarter)
        return pltpu.make_async_copy(x_hbm.at[:, cols], xv.at[:, cols], ld_sem.at[i])

    for i in range(NX):
        load(i).start()
    own_g = pltpu.make_async_copy(g_hbm.at[pl.ds(pl.multiple_of(yh * 256, 256), 256), :], gb.at[0, 0], ld_sem.at[NX])
    own_g.start()

    barrier = pltpu.get_barrier_semaphore()

    def greet(dev):
        pl.semaphore_signal(barrier, inc=1, device_id=dev, device_id_type=MESH)

    y_line = [(a, b, e) for a in range(NH) for b in range(NL) for e in range(NC) if (a, b, e) != (0, 0, 0)]

    def y_dev(a, b, e):
        return {"yh": mod(yh + a, NH), "yl": mod(yl + b, NL), "c": mod(c + e, NC)}

    for k in range(1, NX):
        greet({"x": mod(x + k, NX)})
    for k in range(1, NZ):
        greet({"z": mod(z + k, NZ)})
    for a, b, e in y_line:
        greet(y_dev(a, b, e))
    pl.semaphore_wait(barrier, NX - 1 + NZ - 1 + len(y_line))

    def slab(k):
        return g_hbm.at[pl.ds(pl.multiple_of(mod(k, NH) * 256, 256), 256), :]

    def send_g(p, first=False):
        user = mod(yh - p, NH)
        if not first:
            push(slab(user), gb.at[p, 0], g_ss.at[p, 0], g_rs.at[p, 0], {"yh": user})
        other = {"yh": user, "yl": 1 - yl}
        push(slab(user), gb.at[p, 1], g_ss.at[p, 1], g_rs.at[p, 1], other)
        push(slab(user + 1 - 2 * yl), gb.at[p, 2], g_ss.at[p, 2], g_rs.at[p, 2], other)

    send_g(0, True)

    scales = s_ref[...].astype(F32).T.astype(BF)
    blocks = scales.shape[1]

    def dequant(b):
        pick = (lax.broadcasted_iota(jnp.int32, (blocks, HD), 0) == b).astype(F32).astype(BF)
        spread = jnp.dot(scales, pick, preferred_element_type=F32)
        v = xv[:, pl.ds(pl.multiple_of(b * HD, HD), HD)].astype(F32)
        return (v * spread).astype(BF)

    @pl.loop(0, NX)
    def _(i):
        xq = order_x(i)
        load(i).wait()

        @pl.loop(0, NZ)
        def _(zq):
            par, j = lax.rem(zq, 2), zq // 2
            s = lax.rem(zq + yl, 2)
            b = (xq * NZ + zq) * 2
            xd[c, xq, par, j] = dequant(b + s)
            xs[xq, par, j] = dequant(b + 1 - s)

        push(xd.at[c, xq], xd.at[c, xq], xo_ss.at[xq], xo_rs.at[xq], {"c": 1 - c})
        for par in range(2):
            s_out = lax.rem(par + yl + 1, 2)
            partner = {"yh": mod(yh + s_out * (2 * yl - 1), NH), "yl": 1 - yl}
            push(xs.at[xq, par], xd.at[2 + c, xq, par], xp_ss.at[xq, par], xp_rs.at[xq, par], partner)

    def pass_on(i):
        xq = order_x(i)
        for par in range(2):
            arrived(xd.at[2 + c, xq, par], xp_rs.at[xq, par])
        push(xd.at[2 + c, xq], xd.at[2 + c, xq], xf_ss.at[xq], xf_rs.at[xq], {"c": 1 - c})

    def product(p, xq):
        for par in range(2):
            s = lax.rem(par + yl, 2)
            lhs = jnp.concatenate([gt[0], gt[1 + s]], axis=1)
            for jj in range(2):
                rhs = jnp.concatenate(
                    [
                        jnp.concatenate([xd[k, xq, par, 2 * jj + e] for k in range(4)], axis=0)
                        for e in range(2)
                    ],
                    axis=1,
                )
                res = jnp.dot(lhs, rhs, preferred_element_type=F32).astype(BF)
                for e in range(2):
                    j = 2 * jj + e
                    wx[p, xq, par, j] = res[:RX, e * HD : (e + 1) * HD]
                    wz[p, 2 * j + par, xq] = res[RX:, e * HD : (e + 1) * HD]

    def xdir(par):
        return 1 - 2 * par

    def stage0(p):
        @pl.when(p == 0)
        def _():
            own_g.wait()

        @pl.when(p > 0)
        def _():
            arrived(gb.at[p, 0], g_rs.at[p, 0])

        for k in range(1, 3):
            arrived(gb.at[p, k], g_rs.at[p, k])
        for k in range(3):
            gt[k] = gb[p, k].astype(F32).T.astype(BF)

        @pl.when(p == 0)
        def _():
            pass_on(0)

        @pl.loop(0, NX)
        def _(i):
            xq = order_x(i)

            @pl.when(p == 0)
            def _():
                @pl.when(i < NX - 1)
                def _():
                    pass_on(i + 1)

                arrived(xd.at[1 - c, xq], xo_rs.at[xq])
                arrived(xd.at[3 - c, xq], xf_rs.at[xq])

            product(p, xq)

            @pl.when(i == 0)
            def _():
                for par in range(2):
                    d = xdir(par)
                    push(wx.at[p, xq, par], rxl.at[p, 0, par], xl_ss.at[p, 0, par], xl_rs.at[p, 0, par], {"x": mod(x + d, NX)})

            @pl.when(i == 1)
            def _():
                push(wx.at[p, xq, 1], rxs.at[p, 1], xq_ss.at[p, 1], xq_rs.at[p, 1], {"x": xq})

            @pl.when(i == 2)
            def _():
                push(wx.at[p, xq, 0], rxs.at[p, 0], xq_ss.at[p, 0], xq_rs.at[p, 0], {"x": xq})

            @pl.when((i == 1) & (p < PHASES - 1))
            def _():
                send_g(p + 1)

        for h in range(2):
            z_long(p, 0, h)
            z_short(p, 0, h)

    def z_long(p, k, h):
        d = xdir(h)
        push(
            wz.at[p, mod(z + (4 - k) * d, NZ), pl.ds(2 * h, 2)], rzl.at[p, k, h],
            zl_ss.at[p, k, h], zl_rs.at[p, k, h], {"z": mod(z + d, NZ)},
        )

    def z_short(p, k, h):
        d = xdir(h)
        push(
            wz.at[p, mod(z - (3 - k) * d, NZ), pl.ds(2 * h, 2)], rzs.at[p, k, h],
            zs_ss.at[p, k, h], zs_rs.at[p, k, h], {"z": mod(z - d, NZ)},
        )

    def z_long_add(p, k, h):
        t = mod(z + (3 - k) * xdir(h), NZ)
        arrived(rzl.at[p, k, h], zl_rs.at[p, k, h])
        for e in range(2):
            wz[p, t, 2 * h + e] = (wz[p, t, 2 * h + e].astype(F32) + rzl[p, k, h, e].astype(F32)).astype(BF)
        z_long(p, k + 1, h)

    def z_short_add(p, k, h):
        t = mod(z - (2 - k) * xdir(h), NZ)
        arrived(rzs.at[p, k, h], zs_rs.at[p, k, h])
        for e in range(2):
            wz[p, t, 2 * h + e] = (wz[p, t, 2 * h + e].astype(F32) + rzs[p, k, h, e].astype(F32)).astype(BF)
        z_short(p, k + 1, h)

    def pdir(p):
        return 1 - 2 * lax.rem(p, 2)

    def z2_long(p, k, t):
        push(
            vb.at[p, t], r2zl.at[p, k], z2l_ss.at[p, k], z2l_rs.at[p, k], {"z": mod(z + pdir(p), NZ)}
        )

    def z2_short(p, k, t):
        push(
            vb.at[p, t], r2zs.at[p, k], z2s_ss.at[p, k], z2s_rs.at[p, k], {"z": mod(z - pdir(p), NZ)}
        )

    def z2_long_add(p, k):
        t = mod(z + (3 - k) * pdir(p), NZ)
        arrived(r2zl.at[p, k], z2l_rs.at[p, k])
        vb[p, t] = (vz[p, t] + r2zl[p, k].astype(F32)).astype(BF)
        z2_long(p, k + 1, t)

    def z2_short_add(p, k):
        t = mod(z - (2 - k) * pdir(p), NZ)
        arrived(r2zs.at[p, k], z2s_rs.at[p, k])
        vb[p, t] = (vz[p, t] + r2zs[p, k].astype(F32)).astype(BF)
        z2_short(p, k + 1, t)

    def stage1(p):
        for par in range(2):
            d = xdir(par)
            t = mod(x + d, NX)
            arrived(rxl.at[p, 0, par], xl_rs.at[p, 0, par])
            for j in range(4):
                wx[p, t, par, j] = (wx[p, t, par, j].astype(F32) + rxl[p, 0, par, j].astype(F32)).astype(BF)
            push(wx.at[p, t, par], rxl.at[p, 1, par], xl_ss.at[p, 1, par], xl_rs.at[p, 1, par], {"x": t})
        for h in range(2):
            z_long_add(p, 0, h)
            z_short_add(p, 0, h)

    def stage2(p):
        for par in range(2):
            arrived(rxs.at[p, par], xq_rs.at[p, par])
            arrived(rxl.at[p, 1, par], xl_rs.at[p, 1, par])
            for j in range(4):
                vz[p, 2 * j + par] = (
                    wx[p, x, par, j].astype(F32) + rxs[p, par, j].astype(F32) + rxl[p, 1, par, j].astype(F32)
                )
        d = pdir(p)
        t = mod(z + 4 * d, NZ)
        vb[p, t] = vz[p, t].astype(BF)
        z2_long(p, 0, t)
        t = mod(z - 3 * d, NZ)
        vb[p, t] = vz[p, t].astype(BF)
        z2_short(p, 0, t)
        for h in range(2):
            z_long_add(p, 1, h)
            z_short_add(p, 1, h)

    def stage3(p):
        for h in range(2):
            z_long_add(p, 2, h)
        z2_long_add(p, 0)
        z2_short_add(p, 0)

    def stage4(p):
        for h in range(2):
            arrived(rzs.at[p, 2, h], zs_rs.at[p, 2, h])
            arrived(rzl.at[p, 3, h], zl_rs.at[p, 3, h])
            for e in range(2):
                uz[p, 2 * h + e] = (
                    wz[p, z, 2 * h + e].astype(F32) + rzs[p, 2, h, e].astype(F32) + rzl[p, 3, h, e].astype(F32)
                )
        d = pdir(p)
        t = mod(x + 2 * d, NX)
        ub[p, t] = uz[p, t].astype(BF)
        push(ub.at[p, t], r2xl.at[p, 0], x2l_ss.at[p, 0], x2l_rs.at[p, 0], {"x": mod(x + d, NX)})
        t = mod(x - d, NX)
        ub[p, t] = uz[p, t].astype(BF)
        push(ub.at[p, t], r2xs.at[p], x2s_ss.at[p], x2s_rs.at[p], {"x": t})
        z2_long_add(p, 1)
        z2_short_add(p, 1)

    def stage5(p):
        t = mod(x + pdir(p), NX)
        arrived(r2xl.at[p, 0], x2l_rs.at[p, 0])
        ub[p, t] = (uz[p, t] + r2xl[p, 0].astype(F32)).astype(BF)
        push(ub.at[p, t], r2xl.at[p, 1], x2l_ss.at[p, 1], x2l_rs.at[p, 1], {"x": t})
        z2_long_add(p, 2)

    s_mine = lax.rem(z + yl, 2)
    stays = s_mine == yl

    def stage6(p):
        arrived(r2xs.at[p], x2s_rs.at[p])
        arrived(r2xl.at[p, 1], x2l_rs.at[p, 1])
        arrived(r2zs.at[p, 2], z2s_rs.at[p, 2])
        arrived(r2zl.at[p, 3], z2l_rs.at[p, 3])
        ty[p, :RX] = vz[p, z] + r2zs[p, 2].astype(F32) + r2zl[p, 3].astype(F32)
        ty[p, RX:] = uz[p, x] + r2xs[p].astype(F32) + r2xl[p, 1].astype(F32)
        local = (p == 0) & stays

        @pl.when(local)
        def _():
            ry[0] = ty[0]

        @pl.when(jnp.logical_not(local))
        def _():
            push(ty.at[p], ry.at[p], y_ss.at[p], y_rs.at[p], {"yh": mod(yh + p, NH), "yl": s_mine})

    stages = [stage0, stage1, stage2, stage3, stage4, stage5, stage6]

    @pl.loop(0, STAGES + OFFSET * (PHASES - 1))
    def _(t):
        order = range(STAGES) if NEWEST_FIRST else range(STAGES - 1, -1, -1)
        for k in order:
            ahead = t - k + 8 * OFFSET
            p = ahead // OFFSET - 8

            @pl.when((lax.rem(ahead, OFFSET) == 0) & (p >= 0) & (p < PHASES))
            def _():
                stages[k](p)

    for p in range(1, PHASES):
        arrived(ry.at[p], y_rs.at[p])

    @pl.when(jnp.logical_not(stays))
    def _():
        arrived(ry.at[0], y_rs.at[0])

    total = ry[0] + ry[1] + ry[2] + ry[3]
    out_ref[...] = total.T

    part = jnp.sum((total * total).reshape(16, 8, HD), axis=0)
    nsrc[0] = part
    for k in range(1, NX):
        t = mod(x + k, NX)
        push(nsrc.at[0], n1.at[x], n1_ss.at[t], n1_rs.at[x], {"x": t})
    n1[x] = part
    for k in range(1, NX):
        t = mod(x + k, NX)
        arrived(n1.at[t], n1_rs.at[t])
    part = jnp.sum(n1[...], axis=0)
    nsrc[1] = part
    for k in range(1, NZ):
        t = mod(z + k, NZ)
        push(nsrc.at[1], n2.at[z], n2_ss.at[t], n2_rs.at[z], {"z": t})
    n2[z] = part
    for k in range(1, NZ):
        t = mod(z + k, NZ)
        arrived(n2.at[t], n2_rs.at[t])
    part = jnp.sum(n2[...], axis=0)
    nsrc[2] = part

    def place(h, l, e):
        return (h * NL + l) * NC + e

    mine = place(yh, yl, c)
    for a, b, e in y_line:
        dev = y_dev(a, b, e)
        t = place(dev["yh"], dev["yl"], dev["c"])
        push(nsrc.at[2], n3.at[mine], n3_ss.at[t], n3_rs.at[mine], dev)
    n3[mine] = part
    for a, b, e in y_line:
        dev = y_dev(a, b, e)
        t = place(dev["yh"], dev["yl"], dev["c"])
        arrived(n3.at[t], n3_rs.at[t])
    part = jnp.sum(n3[...], axis=0)
    whole = jnp.sum(jnp.sum(part, axis=1, keepdims=True), axis=0, keepdims=True)
    ss_ref[...] = jnp.broadcast_to(whole, (8, HD))

    for k in range(1, NX):
        t = mod(x + k, NX)
        sent(nsrc.at[0], n1_ss.at[t])
    for k in range(1, NZ):
        t = mod(z + k, NZ)
        sent(nsrc.at[1], n2_ss.at[t])
    for a, b, e in y_line:
        dev = y_dev(a, b, e)
        sent(nsrc.at[2], n3_ss.at[place(dev["yh"], dev["yl"], dev["c"])])

    @pl.when(jnp.logical_not(stays))
    def _():
        sent(ty.at[0], y_ss.at[0])

    @pl.loop(0, PHASES)
    def _(p):
        @pl.when(p > 0)
        def _():
            sent(ty.at[p], y_ss.at[p])
            sent(gb.at[p, 0], g_ss.at[p, 0])

        sent(gb.at[p, 1], g_ss.at[p, 1])
        sent(gb.at[p, 2], g_ss.at[p, 2])
        for h in range(2):
            for k in range(2):
                sent(rxl.at[p, k, h], xl_ss.at[p, k, h])
            sent(rxs.at[p, h], xq_ss.at[p, h])
            for k in range(4):
                sent(rzl.at[p, k, h], zl_ss.at[p, k, h])
            for k in range(3):
                sent(rzs.at[p, k, h], zs_ss.at[p, k, h])
        for k in range(4):
            sent(r2zl.at[p, k], z2l_ss.at[p, k])
        for k in range(3):
            sent(r2zs.at[p, k], z2s_ss.at[p, k])
        for k in range(2):
            sent(r2xl.at[p, k], x2l_ss.at[p, k])
        sent(r2xs.at[p], x2s_ss.at[p])

    @pl.loop(0, NX)
    def _(q):
        sent(xd.at[c, q], xo_ss.at[q])
        sent(xd.at[2 + c, q], xf_ss.at[q])
        for par in range(2):
            sent(xs.at[q, par], xp_ss.at[q, par])


def body(stash_values, stash_scales, value_grad):
    tokens, width = stash_values.shape
    blocks = stash_scales.shape[1]
    dma = pltpu.SemaphoreType.DMA
    pairs = [
        (PHASES, 3), (NX,), (NX, 2), (NX,),
        (PHASES, 2, 2), (PHASES, 2), (PHASES, 4, 2), (PHASES, 3, 2),
        (PHASES, 4), (PHASES, 3), (PHASES, 2), (PHASES,),
        (PHASES,), (NX,), (NZ,), (NH * NL * NC,),
    ]
    total, square = pl.pallas_call(
        kernel,
        out_shape=(
            jax.ShapeDtypeStruct((HD, HD), F32),
            jax.ShapeDtypeStruct((8, HD), F32),
        ),
        in_specs=[
            pl.BlockSpec(memory_space=pl.ANY),
            pl.BlockSpec(memory_space=pltpu.VMEM),
            pl.BlockSpec(memory_space=pl.ANY),
        ],
        out_specs=(
            pl.BlockSpec(memory_space=pltpu.VMEM),
            pl.BlockSpec(memory_space=pltpu.VMEM),
        ),
        scratch_shapes=[
            pltpu.VMEM((tokens, width), BF),
            pltpu.VMEM((4, NX, 2, 4, TOK, HD), BF),
            pltpu.VMEM((NX, 2, 4, TOK, HD), BF),
            pltpu.VMEM((PHASES, 3, 2 * TOK, HD), BF),
            pltpu.VMEM((3, HD, 2 * TOK), BF),
            pltpu.VMEM((PHASES, NX, 2, 4, RX, HD), BF),
            pltpu.VMEM((PHASES, NZ, NX, RZ, HD), BF),
            pltpu.VMEM((PHASES, 2, 2, 4, RX, HD), BF),
            pltpu.VMEM((PHASES, 2, 4, RX, HD), BF),
            pltpu.VMEM((PHASES, 4, 2, 2, RZ, HD), BF),
            pltpu.VMEM((PHASES, 3, 2, 2, RZ, HD), BF),
            pltpu.VMEM((PHASES, NZ, RX, HD), F32),
            pltpu.VMEM((PHASES, NZ, RX, HD), BF),
            pltpu.VMEM((PHASES, NX, RZ, HD), F32),
            pltpu.VMEM((PHASES, NX, RZ, HD), BF),
            pltpu.VMEM((PHASES, 4, RX, HD), BF),
            pltpu.VMEM((PHASES, 3, RX, HD), BF),
            pltpu.VMEM((PHASES, 2, RZ, HD), BF),
            pltpu.VMEM((PHASES, RZ, HD), BF),
            pltpu.VMEM((PHASES, HD, HD), F32),
            pltpu.VMEM((PHASES, HD, HD), F32),
            pltpu.VMEM((3, 8, HD), F32),
            pltpu.VMEM((NX, 8, HD), F32),
            pltpu.VMEM((NZ, 8, HD), F32),
            pltpu.VMEM((NH * NL * NC, 8, HD), F32),
            dma((NX + 1,)),
            *(dma(shape) for pair in pairs for shape in (pair, pair)),
        ],
        compiler_params=pltpu.CompilerParams(
            collective_id=0, has_side_effects=True, vmem_limit_bytes=56 * 1024 * 1024
        ),
    )(stash_values, stash_scales.T, value_grad)
    limit = jnp.sqrt(jnp.float32(width * HD * lax.axis_size("yh") * lax.axis_size("c")))
    return total * jnp.minimum(jnp.float32(1.0), limit / jnp.sqrt(square[0, 0]))


def solution(mesh):
    torus = Mesh(mesh.devices.reshape(NX, NZ, NL, NH, NC), AXES)
    rows = ("x", "z", "yl", "yh", "c")
    return jax.shard_map(
        body,
        mesh=torus,
        in_specs=(P(rows, None), P(rows, None), P(("x", "z", "yl"), ("yh", "c"))),
        out_specs=P(("x", "z", "yl"), ("yh", "c")),
        check_vma=False,
    )
```

```python
import functools
import math

import jax
import jax.numpy as jnp
from jax import lax
from jax.experimental import pallas as pl
from jax.experimental.pallas import tpu as pltpu
from jax.sharding import Mesh
from jax.sharding import PartitionSpec as P

MESH = pl.DeviceIdType.MESH
NX, NZ, NH, NL, NC = 4, 8, 4, 2, 2
AXES = ("x", "z", "yl", "yh", "c")
HD = 128
TOK = 128
RX = 80
RZ = HD - RX
PHASES = NH
SEQUENCE = (
    ("M", 0, 0), ("M", 0, 1), ("xa", 0, 0), ("M", 0, 2), ("xa", 0, 1), ("M", 0, 3), ("G", 1), ("G", 3), ("zl", 0, 0, 0),
    ("zs", 0, 0, 0), ("xb", 0), ("zl", 0, 0, 1), ("zs", 0, 0, 1), ("N", 1), ("G", 2), ("z2l", 0, 0), ("z2s", 0, 0),
    ("zl", 0, 1, 0), ("zs", 0, 1, 0), ("zs", 0, 1, 1), ("zl", 0, 1, 1), ("N", 2), ("z2l", 0, 1), ("z2s", 0, 1),
    ("zl", 0, 2, 0), ("xa", 1, 0), ("xa", 1, 1), ("zl", 1, 0, 0), ("zl", 0, 2, 1), ("zs", 1, 0, 0), ("zl", 1, 0, 1),
    ("zs", 1, 0, 1), ("N", 3), ("z2l", 0, 2), ("zb", 0), ("xa", 2, 0), ("xa", 2, 1), ("zl", 2, 0, 0),
    ("zl", 1, 1, 0), ("zs", 1, 1, 0), ("zs", 2, 0, 0), ("zl", 2, 0, 1), ("zs", 2, 0, 1), ("zl", 1, 1, 1),
    ("zs", 1, 1, 1), ("zl", 3, 0, 0), ("zs", 3, 0, 0), ("zl", 3, 0, 1), ("zs", 3, 0, 1), ("xb", 1), ("zl", 2, 1, 0),
    ("zs", 2, 1, 0), ("zl", 1, 2, 0), ("zl", 2, 1, 1), ("zs", 2, 1, 1), ("zl", 1, 2, 1), ("xa", 3, 0), ("xa", 3, 1),
    ("zs", 3, 1, 0), ("zl", 3, 1, 0), ("zl", 3, 1, 1), ("z2l", 1, 0), ("zs", 3, 1, 1), ("z2s", 1, 0), ("x2a", 0),
    ("zl", 2, 2, 0), ("zl", 2, 2, 1), ("zb", 1), ("xb", 2), ("zl", 3, 2, 0), ("zl", 3, 2, 1), ("z2l", 1, 1),
    ("z2s", 1, 1), ("zb", 2), ("xb", 3), ("f", 0), ("x2a", 1), ("z2l", 2, 0), ("z2s", 2, 0), ("zb", 3),
    ("z2l", 1, 2), ("x2a", 2), ("z2l", 3, 0), ("z2s", 3, 0), ("z2l", 2, 1), ("z2s", 2, 1), ("x2a", 3), ("f", 1),
    ("z2l", 3, 1), ("z2s", 3, 1), ("z2l", 2, 2), ("z2l", 3, 2), ("f", 2), ("f", 3),
)
BF = jnp.bfloat16
F32 = jnp.float32


def mod(value, n):
    return lax.rem(value + 4 * n, n)


def kernel(
    limit, x_hbm, s_hbm, g_hbm, out_ref,
    xv, sv, xd, xs, gb, gt, wx, wz,
    rxl, rxs, rzl, rzs, vz, vb, uz, ub,
    r2zl, r2zs, r2xl, r2xs, ty, ry, nsrc, n1, n2, n3,
    ld_sem, g_ss, g_rs, xo_ss, xo_rs, xp_ss, xp_rs, xf_ss, xf_rs,
    xl_ss, xl_rs, xq_ss, xq_rs, zl_ss, zl_rs, zs_ss, zs_rs,
    z2l_ss, z2l_rs, z2s_ss, z2s_rs, x2l_ss, x2l_rs, x2s_ss, x2s_rs,
    y_ss, y_rs, n1_ss, n1_rs, n2_ss, n2_rs, n3_ss, n3_rs,
):
    x, z, yl, yh, c = (lax.axis_index(name) for name in AXES)
    quarter = NZ * 2 * HD

    def push(src, dst, ss, rs, dev):
        pltpu.make_async_remote_copy(
            src_ref=src, dst_ref=dst, send_sem=ss, recv_sem=rs, device_id=dev, device_id_type=MESH
        ).start()

    def arrived(dst, rs):
        pltpu.make_async_remote_copy(
            src_ref=dst, dst_ref=dst, send_sem=rs, recv_sem=rs, device_id={"c": 1 - c}, device_id_type=MESH
        ).wait_recv()

    def sent(src, ss):
        pltpu.make_async_remote_copy(
            src_ref=src, dst_ref=src, send_sem=ss, recv_sem=ss, device_id={"c": 1 - c}, device_id_type=MESH
        ).wait_send()

    def order_x(i):
        if isinstance(i, int):
            return mod(x + (2, 1, 3, 0)[i], NX)
        return mod(x + jnp.where(i == 0, 2, jnp.where(i == 1, 1, jnp.where(i == 2, 3, 0))), NX)

    def load(i):
        xq = order_x(i)
        cols = pl.ds(pl.multiple_of(xq * quarter, quarter), quarter)
        return pltpu.make_async_copy(x_hbm.at[:, cols], xv.at[:, cols], ld_sem.at[i])

    load(0).start()
    own_g = pltpu.make_async_copy(g_hbm.at[pl.ds(pl.multiple_of(yh * 256, 256), 256), :], gb.at[0, 0], ld_sem.at[NX])
    scale_load = pltpu.make_async_copy(s_hbm, sv, ld_sem.at[NX + 1])
    scale_load.start()

    barrier = pltpu.get_barrier_semaphore()

    def greet(dev):
        pl.semaphore_signal(barrier, inc=1, device_id=dev, device_id_type=MESH)

    x_line = [(k, e) for k in range(NX) for e in range(NC) if (k, e) != (0, 0)]
    y_line = [(a, b) for a in range(NH) for b in range(NL) if (a, b) != (0, 0)]

    def x_dev(k, e):
        return {"x": mod(x + k, NX), "c": mod(c + e, NC)}

    def y_dev(a, b):
        return {"yh": mod(yh + a, NH), "yl": mod(yl + b, NL)}

    for k, e in x_line:
        greet(x_dev(k, e))
    for k in range(1, NZ):
        greet({"z": mod(z + k, NZ)})
    for a, b in y_line:
        greet(y_dev(a, b))

    for i in range(1, NX):
        load(i).start()
    own_g.start()

    def slab(k):
        return g_hbm.at[pl.ds(pl.multiple_of(mod(k, NH) * 256, 256), 256), :]

    beside = {"yl": 1 - yl}
    beyond = {"yh": mod(yh + 2 * yl - 1, NH), "yl": 1 - yl}

    def offset(p):
        if p % 2 == 0:
            return p
        return jnp.where(yl == 1, p, NH - p)

    def send_first_g():
        push(slab(yh), gb.at[0, 1], g_ss.at[0, 1], g_rs.at[0, 1], beside)
        push(slab(yh + 1 - 2 * yl), gb.at[0, 2], g_ss.at[0, 3], g_rs.at[0, 2], beside)

    def send_g(o):
        if o == 0:
            push(slab(yh), gb.at[1 + 2 * yl, 2], g_ss.at[0, 2], g_rs.at[1 + 2 * yl, 2], beyond)
        else:
            user = mod(yh - o, NH)
            push(slab(user), gb.at[o, 0], g_ss.at[o, 0], g_rs.at[o, 0], {"yh": user})

    def op_g(o):
        arrived(gb.at[o, 0], g_rs.at[o, 0])
        push(gb.at[o, 0], gb.at[o, 1], g_ss.at[o, 1], g_rs.at[o, 1], beside)
        other = mod(o + 1 - 2 * yl, NH)

        @pl.when(other > 0)
        def _():
            push(gb.at[o, 0], gb.at[other, 2], g_ss.at[o, 2], g_rs.at[other, 2], beyond)

    scale_load.wait()
    scales = sv[...].astype(F32).T.astype(BF)
    blocks = scales.shape[1]

    def dequant(b):
        pick = (lax.broadcasted_iota(jnp.int32, (blocks, HD), 0) == b).astype(F32).astype(BF)
        spread = jnp.dot(scales, pick, preferred_element_type=F32)
        v = xv[:, pl.ds(pl.multiple_of(b * HD, HD), HD)].astype(F32)
        return (v * spread).astype(BF)

    def prepare(i):
        xq = order_x(i)
        load(i).wait()

        @pl.loop(0, NZ, unroll=4)
        def _(zq):
            par, j = lax.rem(zq, 2), zq // 2
            s = lax.rem(zq + yl, 2)
            b = (xq * NZ + zq) * 2
            xs[xq, par, j] = dequant(b + 1 - s)
            xd[c, xq, par, j] = dequant(b + s)

    def share(i):
        xq = order_x(i)
        for par in range(2):
            s_out = lax.rem(par + yl + 1, 2)
            partner = {"yh": mod(yh + s_out * (2 * yl - 1), NH), "yl": 1 - yl}
            push(xs.at[xq, par], xd.at[2 + c, xq, par], xp_ss.at[xq, par], xp_rs.at[xq, par], partner)
        push(xd.at[c, xq], xd.at[c, xq], xo_ss.at[xq], xo_rs.at[xq], {"c": 1 - c})

    prepare(0)
    pl.semaphore_wait(barrier, len(x_line) + NZ - 1 + len(y_line))
    share(0)
    send_first_g()

    @pl.loop(1, NX)
    def _(i):
        prepare(i)
        share(i)

    near = lax.rem(yl + 1, 2)

    def pass_on(i):
        xq = order_x(i)
        for k in range(2):
            par = lax.rem(near + k, 2)
            arrived(xd.at[2 + c, xq, par], xp_rs.at[xq, par])
            push(xd.at[2 + c, xq, par], xd.at[2 + c, xq, par], xf_ss.at[xq, par], xf_rs.at[xq, par], {"c": 1 - c})

    def product(p, xq):
        for par in range(2):
            s = lax.rem(par + yl, 2)
            lhs = jnp.concatenate([gt[0], gt[1 + s]], axis=1)
            for jj in range(2):
                rhs = jnp.concatenate(
                    [
                        jnp.concatenate([xd[k, xq, par, 2 * jj + e] for k in range(4)], axis=0)
                        for e in range(2)
                    ],
                    axis=1,
                )
                res = jnp.dot(lhs, rhs, preferred_element_type=F32).astype(BF)
                for e in range(2):
                    j = 2 * jj + e
                    wx[p, xq, par, j] = res[:RX, e * HD : (e + 1) * HD]
                    wz[p, 2 * j + par, xq] = res[RX:, e * HD : (e + 1) * HD]

    def xdir(par):
        return 1 - 2 * par

    def after_product(p, i, xq):
        def when(k, run):
            if isinstance(i, int):
                if i == k:
                    run()
            else:
                pl.when(i == k)(run)

        def first():
            for par in range(2):
                d = xdir(par)
                push(wx.at[p, xq, par], rxl.at[p, 0, par], xl_ss.at[p, 0, par], xl_rs.at[p, 0, par], {"x": mod(x + d, NX)})

        def second():
            push(wx.at[p, xq, 1], rxs.at[p, 1], xq_ss.at[p, 1], xq_rs.at[p, 1], {"x": xq})

        def third():
            push(wx.at[p, xq, 0], rxs.at[p, 0], xq_ss.at[p, 0], xq_rs.at[p, 0], {"x": xq})

        when(0, first)
        when(1, second)
        when(2, third)

    def start_z(p):
        for h in range(2):
            z_long(p, 0, h)
            z_short(p, 0, h)

    def take_g(p):
        o = offset(p)
        if p == 0:
            own_g.wait()
        for k in range(1, 3):
            arrived(gb.at[o, k], g_rs.at[o, k])
        for k in range(3):
            gt[k] = gb[o, k].astype(F32).T.astype(BF)

    def op_m(p, i):
        if i == 0:
            pass_on(0)
            take_g(0)
        if i < NX - 1:
            pass_on(i + 1)
        xq = order_x(i)
        arrived(xd.at[1 - c, xq], xo_rs.at[xq])
        for par in range(2):
            arrived(xd.at[3 - c, xq, par], xf_rs.at[xq, par])
        product(p, xq)
        after_product(p, i, xq)
        if i == 1:
            for o in (1, 3, 0):
                send_g(o)
        if i == 2:
            send_g(2)
        if i == NX - 1:
            start_z(p)

    def op_n(p):
        take_g(p)

        @pl.loop(0, NX)
        def _(i):
            xq = order_x(i)
            product(p, xq)
            after_product(p, i, xq)

        start_z(p)

    def z_long(p, k, h):
        d = xdir(h)
        push(
            wz.at[p, mod(z + (4 - k) * d, NZ), pl.ds(2 * h, 2)], rzl.at[p, k, h],
            zl_ss.at[p, k, h], zl_rs.at[p, k, h], {"z": mod(z + d, NZ)},
        )

    def z_short(p, k, h):
        d = xdir(h)
        push(
            wz.at[p, mod(z - (3 - k) * d, NZ), pl.ds(2 * h, 2)], rzs.at[p, k, h],
            zs_ss.at[p, k, h], zs_rs.at[p, k, h], {"z": mod(z - d, NZ)},
        )

    def z_long_add(p, k, h):
        t = mod(z + (3 - k) * xdir(h), NZ)
        arrived(rzl.at[p, k, h], zl_rs.at[p, k, h])
        for e in range(2):
            wz[p, t, 2 * h + e] = (wz[p, t, 2 * h + e].astype(F32) + rzl[p, k, h, e].astype(F32)).astype(BF)
        z_long(p, k + 1, h)

    def z_short_add(p, k, h):
        t = mod(z - (2 - k) * xdir(h), NZ)
        arrived(rzs.at[p, k, h], zs_rs.at[p, k, h])
        for e in range(2):
            wz[p, t, 2 * h + e] = (wz[p, t, 2 * h + e].astype(F32) + rzs[p, k, h, e].astype(F32)).astype(BF)
        z_short(p, k + 1, h)

    def pdir(p):
        return 1 - 2 * (p % 2)

    def z2_long(p, k, t):
        push(
            vb.at[p, t], r2zl.at[p, k], z2l_ss.at[p, k], z2l_rs.at[p, k], {"z": mod(z + pdir(p), NZ)}
        )

    def z2_short(p, k, t):
        push(
            vb.at[p, t], r2zs.at[p, k], z2s_ss.at[p, k], z2s_rs.at[p, k], {"z": mod(z - pdir(p), NZ)}
        )

    def z2_long_add(p, k):
        t = mod(z + (3 - k) * pdir(p), NZ)
        arrived(r2zl.at[p, k], z2l_rs.at[p, k])
        vb[p, t] = (vz[p, t] + r2zl[p, k].astype(F32)).astype(BF)
        z2_long(p, k + 1, t)

    def z2_short_add(p, k):
        t = mod(z - (2 - k) * pdir(p), NZ)
        arrived(r2zs.at[p, k], z2s_rs.at[p, k])
        vb[p, t] = (vz[p, t] + r2zs[p, k].astype(F32)).astype(BF)
        z2_short(p, k + 1, t)

    def op_xa(p, par):
        d = xdir(par)
        t = mod(x + d, NX)
        arrived(rxl.at[p, 0, par], xl_rs.at[p, 0, par])
        for j in range(4):
            wx[p, t, par, j] = (wx[p, t, par, j].astype(F32) + rxl[p, 0, par, j].astype(F32)).astype(BF)
        push(wx.at[p, t, par], rxl.at[p, 1, par], xl_ss.at[p, 1, par], xl_rs.at[p, 1, par], {"x": t})

    def op_xb(p):
        for par in range(2):
            arrived(rxs.at[p, par], xq_rs.at[p, par])
            arrived(rxl.at[p, 1, par], xl_rs.at[p, 1, par])
            for j in range(4):
                vz[p, 2 * j + par] = (
                    wx[p, x, par, j].astype(F32) + rxs[p, par, j].astype(F32) + rxl[p, 1, par, j].astype(F32)
                )
        d = pdir(p)
        t = mod(z + 4 * d, NZ)
        vb[p, t] = vz[p, t].astype(BF)
        z2_long(p, 0, t)
        t = mod(z - 3 * d, NZ)
        vb[p, t] = vz[p, t].astype(BF)
        z2_short(p, 0, t)

    def op_zb(p):
        for h in range(2):
            arrived(rzs.at[p, 2, h], zs_rs.at[p, 2, h])
            arrived(rzl.at[p, 3, h], zl_rs.at[p, 3, h])
            for e in range(2):
                uz[p, 2 * h + e] = (
                    wz[p, z, 2 * h + e].astype(F32) + rzs[p, 2, h, e].astype(F32) + rzl[p, 3, h, e].astype(F32)
                )
        d = pdir(p)
        t = mod(x + 2 * d, NX)
        ub[p, t] = uz[p, t].astype(BF)
        push(ub.at[p, t], r2xl.at[p, 0], x2l_ss.at[p, 0], x2l_rs.at[p, 0], {"x": mod(x + d, NX)})
        t = mod(x - d, NX)
        ub[p, t] = uz[p, t].astype(BF)
        push(ub.at[p, t], r2xs.at[p], x2s_ss.at[p], x2s_rs.at[p], {"x": t})

    def op_x2a(p):
        t = mod(x + pdir(p), NX)
        arrived(r2xl.at[p, 0], x2l_rs.at[p, 0])
        ub[p, t] = (uz[p, t] + r2xl[p, 0].astype(F32)).astype(BF)
        push(ub.at[p, t], r2xl.at[p, 1], x2l_ss.at[p, 1], x2l_rs.at[p, 1], {"x": t})

    s_mine = lax.rem(z + yl, 2)
    stays = s_mine == yl

    def op_f(p):
        arrived(r2xs.at[p], x2s_rs.at[p])
        arrived(r2xl.at[p, 1], x2l_rs.at[p, 1])
        arrived(r2zs.at[p, 2], z2s_rs.at[p, 2])
        arrived(r2zl.at[p, 3], z2l_rs.at[p, 3])
        ty[p, :RX] = vz[p, z] + r2zs[p, 2].astype(F32) + r2zl[p, 3].astype(F32)
        ty[p, RX:] = uz[p, x] + r2xs[p].astype(F32) + r2xl[p, 1].astype(F32)

        def remote():
            o = offset(p)
            push(ty.at[p], ry.at[o], y_ss.at[p], y_rs.at[o], {"yh": mod(yh + o, NH), "yl": s_mine})

        if p > 0:
            remote()
        else:
            pl.when(jnp.logical_not(stays))(remote)

            @pl.when(stays)
            def _():
                ry[0] = ty[0]

    ops = {
        "G": op_g, "M": op_m, "N": op_n, "xa": op_xa, "xb": op_xb, "zl": z_long_add, "zs": z_short_add,
        "z2l": z2_long_add, "z2s": z2_short_add, "zb": op_zb, "x2a": op_x2a, "f": op_f,
    }

    for name, *where in SEQUENCE:
        ops[name](*where)

    def settle(p):
        for k in (1, 2, 3) if p == 0 else (0, 1, 2) if p == 2 else (0, 1):
            sent(gb.at[p, 0], g_ss.at[p, k])
        for h in range(2):
            for k in range(2):
                sent(rxl.at[p, k, h], xl_ss.at[p, k, h])
            sent(rxs.at[p, h], xq_ss.at[p, h])
            for k in range(4):
                sent(rzl.at[p, k, h], zl_ss.at[p, k, h])
            for k in range(3):
                sent(rzs.at[p, k, h], zs_ss.at[p, k, h])
        for k in range(4):
            sent(r2zl.at[p, k], z2l_ss.at[p, k])
        for k in range(3):
            sent(r2zs.at[p, k], z2s_ss.at[p, k])
        for k in range(2):
            sent(r2xl.at[p, k], x2l_ss.at[p, k])
        sent(r2xs.at[p], x2s_ss.at[p])

    for q in range(NX):
        sent(xd.at[c, q], xo_ss.at[q])
        for par in range(2):
            sent(xs.at[q, par], xp_ss.at[q, par])
            sent(xs.at[q, par], xf_ss.at[q, par])
    settle(0)
    sent(gb.at[1, 0], g_ss.at[1 + 2 * yl, 2])

    for p in range(1, PHASES):
        arrived(ry.at[p], y_rs.at[p])

    @pl.when(jnp.logical_not(stays))
    def _():
        arrived(ry.at[0], y_rs.at[0])

    total = ry[0] + ry[1] + ry[2] + ry[3]
    part = jnp.sum(total * total, axis=0, keepdims=True)

    def spot(k, e):
        return mod(x + k, NX) * NC + mod(c + e, NC)

    nsrc[0] = part
    for k, e in x_line:
        push(nsrc.at[0], n1.at[spot(0, 0)], n1_ss.at[spot(k, e)], n1_rs.at[spot(0, 0)], x_dev(k, e))
    n1[spot(0, 0)] = part
    out_ref[...] = total.T
    settle(1)
    for k, e in x_line:
        arrived(n1.at[spot(k, e)], n1_rs.at[spot(k, e)])
    part = jnp.sum(n1[...], axis=0)

    nsrc[1] = part
    for k in range(1, NZ):
        t = mod(z + k, NZ)
        push(nsrc.at[1], n2.at[z], n2_ss.at[t], n2_rs.at[z], {"z": t})
    n2[z] = part
    settle(2)
    for k, e in x_line:
        sent(nsrc.at[0], n1_ss.at[spot(k, e)])
    for k in range(1, NZ):
        t = mod(z + k, NZ)
        arrived(n2.at[t], n2_rs.at[t])
    part = jnp.sum(n2[...], axis=0)

    def place(a, b):
        return mod(yh + a, NH) * NL + mod(yl + b, NL)

    nsrc[2] = part
    for a, b in y_line:
        push(nsrc.at[2], n3.at[place(0, 0)], n3_ss.at[place(a, b)], n3_rs.at[place(0, 0)], y_dev(a, b))
    n3[place(0, 0)] = part
    settle(3)
    for k in range(1, NZ):
        t = mod(z + k, NZ)
        sent(nsrc.at[1], n2_ss.at[t])

    @pl.when(jnp.logical_not(stays))
    def _():
        sent(ty.at[0], y_ss.at[0])

    for p in range(1, PHASES):
        sent(ty.at[p], y_ss.at[p])
    for a, b in y_line:
        arrived(n3.at[place(a, b)], n3_rs.at[place(a, b)])
    part = jnp.sum(n3[...], axis=0)
    whole = jnp.sum(part, axis=1, keepdims=True)
    out_ref[...] = out_ref[...] * jnp.minimum(jnp.float32(1.0), jnp.float32(limit) / jnp.sqrt(whole))
    for a, b in y_line:
        sent(nsrc.at[2], n3_ss.at[place(a, b)])


def body(stash_values, stash_scales, value_grad):
    tokens, width = stash_values.shape
    limit = math.sqrt(width * HD * lax.axis_size("yh") * lax.axis_size("c"))
    dma = pltpu.SemaphoreType.DMA
    pairs = [
        (NH, 4), (NX,), (NX, 2), (NX, 2),
        (PHASES, 2, 2), (PHASES, 2), (PHASES, 4, 2), (PHASES, 3, 2),
        (PHASES, 4), (PHASES, 3), (PHASES, 2), (PHASES,),
        (PHASES,), (NX * NC,), (NZ,), (NH * NL,),
    ]
    return pl.pallas_call(
        functools.partial(kernel, limit),
        out_shape=jax.ShapeDtypeStruct((HD, HD), F32),
        in_specs=[
            pl.BlockSpec(memory_space=pl.ANY),
            pl.BlockSpec(memory_space=pl.ANY),
            pl.BlockSpec(memory_space=pl.ANY),
        ],
        out_specs=pl.BlockSpec(memory_space=pltpu.VMEM),
        scratch_shapes=[
            pltpu.VMEM((tokens, width), BF),
            pltpu.VMEM((stash_scales.shape[1], tokens), BF),
            pltpu.VMEM((4, NX, 2, 4, TOK, HD), BF),
            pltpu.VMEM((NX, 2, 4, TOK, HD), BF),
            pltpu.VMEM((PHASES, 3, 2 * TOK, HD), BF),
            pltpu.VMEM((3, HD, 2 * TOK), BF),
            pltpu.VMEM((PHASES, NX, 2, 4, RX, HD), BF),
            pltpu.VMEM((PHASES, NZ, NX, RZ, HD), BF),
            pltpu.VMEM((PHASES, 2, 2, 4, RX, HD), BF),
            pltpu.VMEM((PHASES, 2, 4, RX, HD), BF),
            pltpu.VMEM((PHASES, 4, 2, 2, RZ, HD), BF),
            pltpu.VMEM((PHASES, 3, 2, 2, RZ, HD), BF),
            pltpu.VMEM((PHASES, NZ, RX, HD), F32),
            pltpu.VMEM((PHASES, NZ, RX, HD), BF),
            pltpu.VMEM((PHASES, NX, RZ, HD), F32),
            pltpu.VMEM((PHASES, NX, RZ, HD), BF),
            pltpu.VMEM((PHASES, 4, RX, HD), BF),
            pltpu.VMEM((PHASES, 3, RX, HD), BF),
            pltpu.VMEM((PHASES, 2, RZ, HD), BF),
            pltpu.VMEM((PHASES, RZ, HD), BF),
            pltpu.VMEM((PHASES, HD, HD), F32),
            pltpu.VMEM((PHASES, HD, HD), F32),
            pltpu.VMEM((3, 1, HD), F32),
            pltpu.VMEM((NX * NC, 1, HD), F32),
            pltpu.VMEM((NZ, 1, HD), F32),
            pltpu.VMEM((NH * NL, 1, HD), F32),
            dma((NX + 2,)),
            *(dma(shape) for pair in pairs for shape in (pair, pair)),
        ],
        compiler_params=pltpu.CompilerParams(
            collective_id=0, has_side_effects=True, vmem_limit_bytes=56 * 1024 * 1024
        ),
    )(stash_values, stash_scales.T, value_grad)


def solution(mesh):
    torus = Mesh(mesh.devices.reshape(NX, NZ, NL, NH, NC), AXES)
    rows = ("x", "z", "yl", "yh", "c")
    return jax.shard_map(
        body,
        mesh=torus,
        in_specs=(P(rows, None), P(rows, None), P(("x", "z", "yl"), ("yh", "c"))),
        out_specs=P(("x", "z", "yl"), ("yh", "c")),
        check_vma=False,
    )
```

```python
import functools
import math

import jax
import jax.numpy as jnp
from jax import lax
from jax.experimental import pallas as pl
from jax.experimental.pallas import tpu as pltpu
from jax.sharding import Mesh
from jax.sharding import PartitionSpec as P

MESH = pl.DeviceIdType.MESH
NX, NZ, NH, NL, NC = 4, 8, 4, 2, 2
AXES = ("x", "z", "yl", "yh", "c")
HD = 128
TOK = 128
RX = 80
RZ = HD - RX
PHASES = NH
SEQUENCE = (
    ("M", 0, 0), ("M", 0, 1), ("xa", 0, 0), ("M", 0, 2), ("xa", 0, 1), ("M", 0, 3), ("G", 1), ("G", 3), ("zl", 0, 0, 0),
    ("zs", 0, 0, 0), ("xb", 0), ("zl", 0, 0, 1), ("zs", 0, 0, 1), ("N", 1), ("G", 2), ("z2l", 0, 0), ("z2s", 0, 0),
    ("zl", 0, 1, 0), ("zs", 0, 1, 0), ("zs", 0, 1, 1), ("zl", 0, 1, 1), ("N", 2), ("z2l", 0, 1), ("z2s", 0, 1),
    ("zl", 0, 2, 0), ("xa", 1, 0), ("xa", 1, 1), ("zl", 1, 0, 0), ("zl", 0, 2, 1), ("zs", 1, 0, 0), ("zl", 1, 0, 1),
    ("zs", 1, 0, 1), ("N", 3), ("z2l", 0, 2), ("zb", 0), ("xa", 2, 0), ("xa", 2, 1), ("zl", 2, 0, 0),
    ("zl", 1, 1, 0), ("zs", 1, 1, 0), ("zs", 2, 0, 0), ("zl", 2, 0, 1), ("zs", 2, 0, 1), ("zl", 1, 1, 1),
    ("zs", 1, 1, 1), ("zl", 3, 0, 0), ("zs", 3, 0, 0), ("zl", 3, 0, 1), ("zs", 3, 0, 1), ("xb", 1), ("zl", 2, 1, 0),
    ("zs", 2, 1, 0), ("zl", 1, 2, 0), ("zl", 2, 1, 1), ("zs", 2, 1, 1), ("zl", 1, 2, 1), ("xa", 3, 0), ("xa", 3, 1),
    ("zs", 3, 1, 0), ("zl", 3, 1, 0), ("zl", 3, 1, 1), ("z2l", 1, 0), ("zs", 3, 1, 1), ("z2s", 1, 0), ("x2a", 0),
    ("zl", 2, 2, 0), ("zl", 2, 2, 1), ("zb", 1), ("xb", 2), ("zl", 3, 2, 0), ("zl", 3, 2, 1), ("z2l", 1, 1),
    ("z2s", 1, 1), ("zb", 2), ("xb", 3), ("f", 0), ("x2a", 1), ("z2l", 2, 0), ("z2s", 2, 0), ("zb", 3),
    ("z2l", 1, 2), ("x2a", 2), ("z2l", 3, 0), ("z2s", 3, 0), ("z2l", 2, 1), ("z2s", 2, 1), ("x2a", 3), ("f", 1),
    ("z2l", 3, 1), ("z2s", 3, 1), ("z2l", 2, 2), ("z2l", 3, 2), ("f", 2), ("f", 3),
)
BF = jnp.bfloat16
F32 = jnp.float32


def mod(value, n):
    return lax.rem(value + 4 * n, n)


def kernel(
    limit, x_hbm, s_hbm, g_hbm, out_ref,
    xv, sv, xd, xs, gb, gt, wx, wz,
    rxl, rxb, rzl, rzs, rzf, vz, vb, uz, ub,
    r2zl, r2zs, r2x, f2z, f2x, ty, ry, nsrc, n1, n2, n3,
    ld_sem, out_sem, rs_sem, g_own, g_rs, xo_rs, xp_rs, xf_rs,
    xl_rs, xb_rs, zl_rs, zs_rs, zf_rs, z2l_rs, z2s_rs, x2_rs, fz_rs, fx_rs,
    y_rs, n_rs,
):
    x, z, yl, yh, c = (lax.axis_index(name) for name in AXES)
    quarter = NZ * 2 * HD

    def push(src, dst, ss, rs, dev):
        pltpu.make_async_remote_copy(
            src_ref=src, dst_ref=dst, send_sem=ss, recv_sem=rs, device_id=dev, device_id_type=MESH
        ).start()

    def arrived(dst, rs):
        pltpu.make_async_remote_copy(
            src_ref=dst, dst_ref=dst, send_sem=rs, recv_sem=rs, device_id={"c": 1 - c}, device_id_type=MESH
        ).wait_recv()

    def sent(src, ss):
        pltpu.make_async_remote_copy(
            src_ref=src, dst_ref=src, send_sem=ss, recv_sem=ss, device_id={"c": 1 - c}, device_id_type=MESH
        ).wait_send()

    def order_x(i):
        if isinstance(i, int):
            return mod(x + (2, 1, 3, 0)[i], NX)
        return mod(x + jnp.where(i == 0, 2, jnp.where(i == 1, 1, jnp.where(i == 2, 3, 0))), NX)

    def load(i):
        xq = order_x(i)
        cols = pl.ds(pl.multiple_of(xq * quarter, quarter), quarter)
        return pltpu.make_async_copy(x_hbm.at[:, cols], xv.at[:, cols], ld_sem.at[i])

    load(0).start()
    own_g = pltpu.make_async_copy(g_hbm.at[pl.ds(pl.multiple_of(yh * 256, 256), 256), :], gb.at[0, 0], ld_sem.at[NX])
    scale_load = pltpu.make_async_copy(s_hbm, sv, ld_sem.at[NX + 1])
    scale_load.start()

    barrier = pltpu.get_barrier_semaphore()

    def greet(dev):
        pl.semaphore_signal(barrier, inc=1, device_id=dev, device_id_type=MESH)

    x_line = [(k, e) for k in range(NX) for e in range(NC) if (k, e) != (0, 0)]
    y_line = [(a, b) for a in range(NH) for b in range(NL) if (a, b) != (0, 0)]

    def x_dev(k, e):
        return {"x": mod(x + k, NX), "c": mod(c + e, NC)}

    def y_dev(a, b):
        return {"yh": mod(yh + a, NH), "yl": mod(yl + b, NL)}

    for k, e in x_line:
        greet(x_dev(k, e))
    for k in range(1, NZ):
        greet({"z": mod(z + k, NZ)})
    for a, b in y_line:
        greet(y_dev(a, b))

    for i in range(1, NX):
        load(i).start()
    own_g.start()

    def slab(k):
        return g_hbm.at[pl.ds(pl.multiple_of(mod(k, NH) * 256, 256), 256), :]

    beside = {"yl": 1 - yl}
    beyond = {"yh": mod(yh + 2 * yl - 1, NH), "yl": 1 - yl}

    def offset(p):
        if p % 2 == 0:
            return p
        return jnp.where(yl == 1, p, NH - p)

    def send_first_g():
        push(slab(yh), gb.at[0, 1], out_sem.at[1], g_rs.at[0], beside)
        push(slab(yh + 1 - 2 * yl), gb.at[0, 2], out_sem.at[1], g_rs.at[0], beside)

    def send_g(o):
        if o == 0:
            push(slab(yh), gb.at[1 + 2 * yl, 2], out_sem.at[1], g_rs.at[1 + 2 * yl], beyond)
        else:
            user = mod(yh - o, NH)
            push(slab(user), gb.at[o, 0], out_sem.at[1], g_own.at[o], {"yh": user})

    def op_g(o):
        arrived(gb.at[o, 0], g_own.at[o])
        push(gb.at[o, 0], gb.at[o, 1], out_sem.at[1], g_rs.at[o], beside)
        other = mod(o + 1 - 2 * yl, NH)

        @pl.when(other > 0)
        def _():
            push(gb.at[o, 0], gb.at[other, 2], out_sem.at[1], g_rs.at[other], beyond)

    scale_load.wait()
    scales = sv[...].astype(F32).T.astype(BF)
    blocks = scales.shape[1]

    def dequant(b):
        pick = (lax.broadcasted_iota(jnp.int32, (blocks, HD), 0) == b).astype(F32).astype(BF)
        spread = jnp.dot(scales, pick, preferred_element_type=F32)
        v = xv[:, pl.ds(pl.multiple_of(b * HD, HD), HD)].astype(F32)
        return (v * spread).astype(BF)

    def prepare(i):
        xq = order_x(i)
        load(i).wait()

        @pl.loop(0, NZ, unroll=4)
        def _(zq):
            par, j = lax.rem(zq, 2), zq // 2
            s = lax.rem(zq + yl, 2)
            b = (xq * NZ + zq) * 2
            xs[xq * 8 + par * 4 + j] = dequant(b + 1 - s)
            xd[c, xq, par, j] = dequant(b + s)

    def share(i):
        xq = order_x(i)
        for par in range(2):
            s_out = lax.rem(par + yl + 1, 2)
            partner = {"yh": mod(yh + s_out * (2 * yl - 1), NH), "yl": 1 - yl}
            push(xs.at[pl.ds(xq * 8 + par * 4, 4)], xd.at[2 + c, xq, par], out_sem.at[0], xp_rs.at[xq, par], partner)

    def share_chip(i):
        xq = order_x(i)
        push(xd.at[c, xq], xd.at[c, xq], out_sem.at[0], xo_rs.at[xq], {"c": 1 - c})

    prepare(0)
    pl.semaphore_wait(barrier, len(x_line) + NZ - 1 + len(y_line))
    share(0)
    send_first_g()
    share_chip(0)

    @pl.loop(1, NX)
    def _(i):
        prepare(i)
        share(i)

    near = lax.rem(yl + 1, 2)

    def pass_on(i):
        xq = order_x(i)
        for k in range(2):
            par = lax.rem(near + k, 2)
            arrived(xd.at[2 + c, xq, par], xp_rs.at[xq, par])
            push(xd.at[2 + c, xq, par], xd.at[2 + c, xq, par], out_sem.at[0], xf_rs.at[xq], {"c": 1 - c})

    def product(p, xq):
        for par in range(2):
            s = lax.rem(par + yl, 2)
            lhs = jnp.concatenate([gt[0], gt[1 + s]], axis=1)
            for jj in range(2):
                rhs = jnp.concatenate(
                    [
                        jnp.concatenate([xd[k, xq, par, 2 * jj + e] for k in range(4)], axis=0)
                        for e in range(2)
                    ],
                    axis=1,
                )
                res = jnp.dot(lhs, rhs, preferred_element_type=F32).astype(BF)
                for e in range(2):
                    j = 2 * jj + e
                    wx[p, xq, par, j] = res[:RX, e * HD : (e + 1) * HD]
                    wz[p, 2 * j + par, xq] = res[RX:, e * HD : (e + 1) * HD]

    def xdir(par):
        return 1 - 2 * par

    def after_product(p, i, xq):
        def when(k, run):
            if isinstance(i, int):
                if i == k:
                    run()
            else:
                pl.when(i == k)(run)

        def first():
            for par in range(2):
                d = xdir(par)
                push(wx.at[p, xq, par], rxl.at[p, par], rs_sem.at[p], xl_rs.at[p, par], {"x": mod(x + d, NX)})

        def second():
            push(wx.at[p, xq, 1], rxb.at[p, 3], rs_sem.at[p], xb_rs.at[p], {"x": xq})

        def third():
            push(wx.at[p, xq, 0], rxb.at[p, 2], rs_sem.at[p], xb_rs.at[p], {"x": xq})

        when(0, first)
        when(1, second)
        when(2, third)

    def start_z(p):
        for h in range(2):
            z_long(p, 0, h)
            z_short(p, 0, h)

    def take_g(p):
        o = offset(p)
        if p == 0:
            own_g.wait()
        arrived(gb.at[o, pl.ds(1, 2)], g_rs.at[o])
        for k in range(3):
            gt[k] = gb[o, k].astype(F32).T.astype(BF)

    def op_m(p, i):
        if i == 0:
            pass_on(0)
            share_chip(1)
            take_g(0)
        xq = order_x(i)
        arrived(xd.at[1 - c, xq], xo_rs.at[xq])
        arrived(xd.at[3 - c, xq], xf_rs.at[xq])
        product(p, xq)
        after_product(p, i, xq)
        if i < NX - 1:
            pass_on(i + 1)
            if i < NX - 2:
                share_chip(i + 2)
        if i == 1:
            for o in (1, 3, 0):
                send_g(o)
        if i == 2:
            send_g(2)
        if i == NX - 1:
            start_z(p)

    def op_n(p):
        take_g(p)

        @pl.loop(0, NX)
        def _(i):
            xq = order_x(i)
            product(p, xq)
            after_product(p, i, xq)

        start_z(p)

    def z_long(p, k, h):
        d = xdir(h)
        dst, rs = (rzf.at[p, h], zf_rs.at[p]) if k == 3 else (rzl.at[p, k, h], zl_rs.at[p, k, h])
        src = wz.at[p, mod(z + (4 - k) * d, NZ), pl.ds(2 * h, 2)]
        push(src, dst, rs_sem.at[p], rs, {"z": mod(z + d, NZ)})

    def z_short(p, k, h):
        d = xdir(h)
        dst, rs = (rzf.at[p, 2 + h], zf_rs.at[p]) if k == 2 else (rzs.at[p, k, h], zs_rs.at[p, k, h])
        src = wz.at[p, mod(z - (3 - k) * d, NZ), pl.ds(2 * h, 2)]
        push(src, dst, rs_sem.at[p], rs, {"z": mod(z - d, NZ)})

    def z_long_add(p, k, h):
        t = mod(z + (3 - k) * xdir(h), NZ)
        arrived(rzl.at[p, k, h], zl_rs.at[p, k, h])
        for e in range(2):
            wz[p, t, 2 * h + e] = (wz[p, t, 2 * h + e].astype(F32) + rzl[p, k, h, e].astype(F32)).astype(BF)
        z_long(p, k + 1, h)

    def z_short_add(p, k, h):
        t = mod(z - (2 - k) * xdir(h), NZ)
        arrived(rzs.at[p, k, h], zs_rs.at[p, k, h])
        for e in range(2):
            wz[p, t, 2 * h + e] = (wz[p, t, 2 * h + e].astype(F32) + rzs[p, k, h, e].astype(F32)).astype(BF)
        z_short(p, k + 1, h)

    def pdir(p):
        return 1 - 2 * (p % 2)

    def z2_long(p, k, t):
        dst, rs = (f2z.at[p, 0], fz_rs.at[p]) if k == 3 else (r2zl.at[p, k], z2l_rs.at[p, k])
        push(vb.at[p, t], dst, rs_sem.at[p], rs, {"z": mod(z + pdir(p), NZ)})

    def z2_short(p, k, t):
        dst, rs = (f2z.at[p, 1], fz_rs.at[p]) if k == 2 else (r2zs.at[p, k], z2s_rs.at[p, k])
        push(vb.at[p, t], dst, rs_sem.at[p], rs, {"z": mod(z - pdir(p), NZ)})

    def z2_long_add(p, k):
        t = mod(z + (3 - k) * pdir(p), NZ)
        arrived(r2zl.at[p, k], z2l_rs.at[p, k])
        vb[p, t] = (vz[p, t] + r2zl[p, k].astype(F32)).astype(BF)
        z2_long(p, k + 1, t)

    def z2_short_add(p, k):
        t = mod(z - (2 - k) * pdir(p), NZ)
        arrived(r2zs.at[p, k], z2s_rs.at[p, k])
        vb[p, t] = (vz[p, t] + r2zs[p, k].astype(F32)).astype(BF)
        z2_short(p, k + 1, t)

    def op_xa(p, par):
        d = xdir(par)
        t = mod(x + d, NX)
        arrived(rxl.at[p, par], xl_rs.at[p, par])
        for j in range(4):
            wx[p, t, par, j] = (wx[p, t, par, j].astype(F32) + rxl[p, par, j].astype(F32)).astype(BF)
        push(wx.at[p, t, par], rxb.at[p, par], rs_sem.at[p], xb_rs.at[p], {"x": t})

    def op_xb(p):
        arrived(rxb.at[p], xb_rs.at[p])
        for par in range(2):
            for j in range(4):
                vz[p, 2 * j + par] = (
                    wx[p, x, par, j].astype(F32) + rxb[p, 2 + par, j].astype(F32) + rxb[p, par, j].astype(F32)
                )
        d = pdir(p)
        t = mod(z + 4 * d, NZ)
        vb[p, t] = vz[p, t].astype(BF)
        z2_long(p, 0, t)
        t = mod(z - 3 * d, NZ)
        vb[p, t] = vz[p, t].astype(BF)
        z2_short(p, 0, t)

    def op_zb(p):
        arrived(rzf.at[p], zf_rs.at[p])
        for h in range(2):
            for e in range(2):
                uz[p, 2 * h + e] = (
                    wz[p, z, 2 * h + e].astype(F32) + rzf[p, 2 + h, e].astype(F32) + rzf[p, h, e].astype(F32)
                )
        d = pdir(p)
        t = mod(x + 2 * d, NX)
        ub[p, t] = uz[p, t].astype(BF)
        push(ub.at[p, t], r2x.at[p], rs_sem.at[p], x2_rs.at[p], {"x": mod(x + d, NX)})
        t = mod(x - d, NX)
        ub[p, t] = uz[p, t].astype(BF)
        push(ub.at[p, t], f2x.at[p, 1], rs_sem.at[p], fx_rs.at[p], {"x": t})

    def op_x2a(p):
        t = mod(x + pdir(p), NX)
        arrived(r2x.at[p], x2_rs.at[p])
        ub[p, t] = (uz[p, t] + r2x[p].astype(F32)).astype(BF)
        push(ub.at[p, t], f2x.at[p, 0], rs_sem.at[p], fx_rs.at[p], {"x": t})

    s_mine = lax.rem(z + yl, 2)
    stays = s_mine == yl

    def op_f(p):
        arrived(f2x.at[p], fx_rs.at[p])
        arrived(f2z.at[p], fz_rs.at[p])
        ty[p, :RX] = vz[p, z] + f2z[p, 0].astype(F32) + f2z[p, 1].astype(F32)
        ty[p, RX:] = uz[p, x] + f2x[p, 0].astype(F32) + f2x[p, 1].astype(F32)
        far = 1 if p > 0 else 0

        def remote():
            o = offset(p)
            push(ty.at[p], ry.at[o], out_sem.at[2 + far], y_rs.at[far], {"yh": mod(yh + o, NH), "yl": s_mine})

        if p > 0:
            remote()
        else:
            pl.when(jnp.logical_not(stays))(remote)

            @pl.when(stays)
            def _():
                ry[0] = ty[0]

    ops = {
        "G": op_g, "M": op_m, "N": op_n, "xa": op_xa, "xb": op_xb, "zl": z_long_add, "zs": z_short_add,
        "z2l": z2_long_add, "z2s": z2_short_add, "zb": op_zb, "x2a": op_x2a, "f": op_f,
    }

    for name, *where in SEQUENCE:
        ops[name](*where)

    sent(xd.at[pl.ds(0, 3)], out_sem.at[0])
    sent(xs.at[pl.ds(0, 22)], out_sem.at[1])
    for p in range(PHASES):
        sent(xs.at[pl.ds(0, 31)], rs_sem.at[p])
    arrived(ry.at[pl.ds(1, PHASES - 1)], y_rs.at[1])

    @pl.when(jnp.logical_not(stays))
    def _():
        arrived(ry.at[0], y_rs.at[0])

    total = ry[0] + ry[1] + ry[2] + ry[3]
    part = jnp.sum(total * total, axis=0, keepdims=True)

    def spot(k, e):
        return mod(x + k, NX) * NC + mod(c + e, NC)

    nsrc[0] = part
    for k, e in x_line:
        push(nsrc.at[0], n1.at[spot(0, 0)], out_sem.at[4], n_rs.at[0], x_dev(k, e))
    n1[spot(0, 0)] = part
    out_ref[...] = total.T
    arrived(n1.at[pl.ds(0, len(x_line))], n_rs.at[0])
    part = jnp.sum(n1[...], axis=0)

    nsrc[1] = part
    for k in range(1, NZ):
        t = mod(z + k, NZ)
        push(nsrc.at[1], n2.at[z], out_sem.at[5], n_rs.at[1], {"z": t})
    n2[z] = part
    sent(n1.at[pl.ds(0, len(x_line))], out_sem.at[4])
    arrived(n2.at[pl.ds(0, NZ - 1)], n_rs.at[1])
    part = jnp.sum(n2[...], axis=0)

    def place(a, b):
        return mod(yh + a, NH) * NL + mod(yl + b, NL)

    nsrc[2] = part
    for a, b in y_line:
        push(nsrc.at[2], n3.at[place(0, 0)], out_sem.at[6], n_rs.at[2], y_dev(a, b))
    n3[place(0, 0)] = part
    sent(n2.at[pl.ds(0, NZ - 1)], out_sem.at[5])

    @pl.when(jnp.logical_not(stays))
    def _():
        sent(ty.at[0], out_sem.at[2])

    sent(ty.at[pl.ds(1, PHASES - 1)], out_sem.at[3])
    arrived(n3.at[pl.ds(0, len(y_line))], n_rs.at[2])
    part = jnp.sum(n3[...], axis=0)
    whole = jnp.sum(part, axis=1, keepdims=True)
    out_ref[...] = out_ref[...] * jnp.minimum(jnp.float32(1.0), jnp.float32(limit) / jnp.sqrt(whole))
    sent(n3.at[pl.ds(0, len(y_line))], out_sem.at[6])


def body(stash_values, stash_scales, value_grad):
    tokens, width = stash_values.shape
    limit = math.sqrt(width * HD * lax.axis_size("yh") * lax.axis_size("c"))
    dma = pltpu.SemaphoreType.DMA
    return pl.pallas_call(
        functools.partial(kernel, limit),
        out_shape=jax.ShapeDtypeStruct((HD, HD), F32),
        in_specs=[
            pl.BlockSpec(memory_space=pl.ANY),
            pl.BlockSpec(memory_space=pl.ANY),
            pl.BlockSpec(memory_space=pl.ANY),
        ],
        out_specs=pl.BlockSpec(memory_space=pltpu.VMEM),
        scratch_shapes=[
            pltpu.VMEM((tokens, width), BF),
            pltpu.VMEM((stash_scales.shape[1], tokens), BF),
            pltpu.VMEM((4, NX, 2, 4, TOK, HD), BF),
            pltpu.VMEM((NX * 8, TOK, HD), BF),
            pltpu.VMEM((NH, 3, 2 * TOK, HD), BF),
            pltpu.VMEM((3, HD, 2 * TOK), BF),
            pltpu.VMEM((PHASES, NX, 2, 4, RX, HD), BF),
            pltpu.VMEM((PHASES, NZ, NX, RZ, HD), BF),
            pltpu.VMEM((PHASES, 2, 4, RX, HD), BF),
            pltpu.VMEM((PHASES, 4, 4, RX, HD), BF),
            pltpu.VMEM((PHASES, 3, 2, 2, RZ, HD), BF),
            pltpu.VMEM((PHASES, 2, 2, 2, RZ, HD), BF),
            pltpu.VMEM((PHASES, 4, 2, RZ, HD), BF),
            pltpu.VMEM((PHASES, NZ, RX, HD), F32),
            pltpu.VMEM((PHASES, NZ, RX, HD), BF),
            pltpu.VMEM((PHASES, NX, RZ, HD), F32),
            pltpu.VMEM((PHASES, NX, RZ, HD), BF),
            pltpu.VMEM((PHASES, 3, RX, HD), BF),
            pltpu.VMEM((PHASES, 2, RX, HD), BF),
            pltpu.VMEM((PHASES, RZ, HD), BF),
            pltpu.VMEM((PHASES, 2, RX, HD), BF),
            pltpu.VMEM((PHASES, 2, RZ, HD), BF),
            pltpu.VMEM((PHASES, HD, HD), F32),
            pltpu.VMEM((PHASES, HD, HD), F32),
            pltpu.VMEM((3, 1, HD), F32),
            pltpu.VMEM((NX * NC, 1, HD), F32),
            pltpu.VMEM((NZ, 1, HD), F32),
            pltpu.VMEM((NH * NL, 1, HD), F32),
            dma((NX + 2,)),
            dma((7,)),
            dma((PHASES,)),
            dma((NH,)),
            dma((NH,)),
            dma((NX,)),
            dma((NX, 2)),
            dma((NX,)),
            dma((PHASES, 2)),
            dma((PHASES,)),
            dma((PHASES, 3, 2)),
            dma((PHASES, 2, 2)),
            dma((PHASES,)),
            dma((PHASES, 3)),
            dma((PHASES, 2)),
            dma((PHASES,)),
            dma((PHASES,)),
            dma((PHASES,)),
            dma((2,)),
            dma((3,)),
        ],
        compiler_params=pltpu.CompilerParams(
            collective_id=0, has_side_effects=True, vmem_limit_bytes=56 * 1024 * 1024
        ),
    )(stash_values, stash_scales.T, value_grad)


def solution(mesh):
    torus = Mesh(mesh.devices.reshape(NX, NZ, NL, NH, NC), AXES)
    rows = ("x", "z", "yl", "yh", "c")
    return jax.shard_map(
        body,
        mesh=torus,
        in_specs=(P(rows, None), P(rows, None), P(("x", "z", "yl"), ("yh", "c"))),
        out_specs=P(("x", "z", "yl"), ("yh", "c")),
        check_vma=False,
    )
```

```python
import functools
import math

import jax
import jax.numpy as jnp
from jax import lax
from jax.experimental import pallas as pl
from jax.experimental.pallas import tpu as pltpu
from jax.sharding import Mesh
from jax.sharding import PartitionSpec as P

MESH = pl.DeviceIdType.MESH
NX, NZ, NH, NL, NC = 4, 8, 4, 2, 2
AXES = ("x", "z", "yl", "yh", "c")
HD = 128
TOK = 128
ROWS = (80, 80, 80, 80)
PHASES = NH
TREE = (2, 3)
SEQUENCE = (
    ("M", 0, 0), ("M", 0, 1), ("xa", 0, 0), ("M", 0, 2), ("G", 0), ("xa", 0, 1), ("M", 0, 3), ("G", 1), ("G", 2),
    ("zl", 0, 0, 0), ("zs", 0, 0, 0), ("N", 1), ("G", 3), ("G", 4), ("xb", 0), ("zl", 0, 1, 0), ("zs", 0, 1, 0),
    ("zl", 0, 0, 1), ("zs", 0, 0, 1), ("N", 2), ("z2l", 0, 0), ("z2s", 0, 0), ("zl", 0, 2, 0), ("xa", 1, 0),
    ("xa", 1, 1), ("zl", 0, 1, 1), ("zs", 0, 1, 1), ("zl", 1, 0, 0), ("zs", 1, 0, 0), ("zl", 1, 0, 1),
    ("zs", 1, 0, 1), ("N", 3), ("zl", 2, 0, 0), ("z2l", 0, 1), ("z2s", 0, 1), ("xa", 2, 0), ("xa", 2, 1),
    ("zs", 2, 0, 0), ("zl", 0, 2, 1), ("zl", 2, 0, 1), ("zs", 2, 0, 1), ("zs", 1, 1, 0), ("zl", 1, 1, 0),
    ("zl", 1, 1, 1), ("zs", 1, 1, 1), ("zs", 3, 0, 0), ("zl", 3, 0, 0), ("zl", 3, 0, 1), ("zs", 3, 0, 1),
    ("zs", 2, 1, 0), ("zl", 2, 1, 0), ("xb", 1), ("z2l", 0, 2), ("zb", 0), ("zs", 2, 1, 1), ("zl", 2, 1, 1),
    ("zl", 1, 2, 0), ("xa", 3, 0), ("xa", 3, 1), ("zl", 1, 2, 1), ("zl", 3, 1, 0), ("zs", 3, 1, 0), ("zs", 3, 1, 1),
    ("zl", 3, 1, 1), ("zl", 2, 2, 0), ("z2s", 1, 0), ("z2l", 1, 0), ("fz", 0), ("zl", 2, 2, 1), ("xb", 2),
    ("x2a", 0), ("zb", 1), ("zl", 3, 2, 0), ("zl", 3, 2, 1), ("z2l", 1, 1), ("zb", 2), ("xb", 3), ("fx", 0),
    ("x2a", 1), ("z2s", 1, 1), ("zt", 2, 0), ("zt", 2, 2), ("zt", 2, 1), ("zb", 3), ("z2l", 1, 2), ("x2a", 2),
    ("zt", 3, 0), ("zt", 3, 2), ("fx", 1), ("zt", 3, 1), ("x2a", 3), ("fx", 2), ("fz", 1), ("fz", 2), ("fx", 3),
    ("fz", 3),
)
BF = jnp.bfloat16
F32 = jnp.float32


def mod(value, n):
    return lax.rem(value + 4 * n, n)


def kernel(
    limit, x_hbm, s_hbm, g_hbm, out_ref, *scratch
):
    x, z, yl, yh, c = (lax.axis_index(name) for name in AXES)
    quarter = NZ * 2 * HD
    xv, sv, xd, xs, gb, gt, ty, ry, nsrc, n1, n2, n3 = scratch[:12]
    (
        ld_sem, out_sem, rs_sem, g_own, g_rs, xo_rs, xp_rs, xf_rs,
        xl_rs, xb_rs, zl_rs, zs_rs, zf_rs, z2l_rs, z2s_rs, x2_rs, fz_rs, fx_rs,
        y_rs, n_rs,
    ) = scratch[12:32]
    (
        wx, wz, rxl, rxb, rzl, rzs, rzf, vz, vb, uz, ub, r2zl, r2zs, r2x, f2z, f2x,
    ) = (scratch[32 + k :: 16] for k in range(16))

    def push(src, dst, ss, rs, dev):
        pltpu.make_async_remote_copy(
            src_ref=src, dst_ref=dst, send_sem=ss, recv_sem=rs, device_id=dev, device_id_type=MESH
        ).start()

    def arrived(dst, rs):
        pltpu.make_async_remote_copy(
            src_ref=dst, dst_ref=dst, send_sem=rs, recv_sem=rs, device_id={"c": 1 - c}, device_id_type=MESH
        ).wait_recv()

    def sent(src, ss):
        pltpu.make_async_remote_copy(
            src_ref=src, dst_ref=src, send_sem=ss, recv_sem=ss, device_id={"c": 1 - c}, device_id_type=MESH
        ).wait_send()

    def order_x(i):
        if isinstance(i, int):
            return mod(x + (2, 1, 3, 0)[i], NX)
        return mod(x + jnp.where(i == 0, 2, jnp.where(i == 1, 1, jnp.where(i == 2, 3, 0))), NX)

    def load(i):
        xq = order_x(i)
        cols = pl.ds(pl.multiple_of(xq * quarter, quarter), quarter)
        return pltpu.make_async_copy(x_hbm.at[:, cols], xv.at[:, cols], ld_sem.at[i])

    load(0).start()
    own_g = pltpu.make_async_copy(g_hbm.at[pl.ds(pl.multiple_of(yh * 256, 256), 256), :], gb.at[0, 0], ld_sem.at[NX])
    scale_load = pltpu.make_async_copy(s_hbm, sv, ld_sem.at[NX + 1])
    scale_load.start()

    barrier = pltpu.get_barrier_semaphore()

    def greet(dev):
        pl.semaphore_signal(barrier, inc=1, device_id=dev, device_id_type=MESH)

    x_line = [(k, e) for k in range(NX) for e in range(NC) if (k, e) != (0, 0)]
    y_line = [(a, b) for a in range(NH) for b in range(NL) if (a, b) != (0, 0)]

    def x_dev(k, e):
        return {"x": mod(x + k, NX), "c": mod(c + e, NC)}

    def y_dev(a, b):
        return {"yh": mod(yh + a, NH), "yl": mod(yl + b, NL)}

    for k, e in x_line:
        greet(x_dev(k, e))
    for k in range(1, NZ):
        greet({"z": mod(z + k, NZ)})
    for a, b in y_line:
        greet(y_dev(a, b))

    for i in range(1, NX):
        load(i).start()
    own_g.start()

    def slab(k):
        return g_hbm.at[pl.ds(pl.multiple_of(mod(k, NH) * 256, 256), 256), :]

    beside = {"yl": 1 - yl}
    beyond = {"yh": mod(yh + 2 * yl - 1, NH), "yl": 1 - yl}

    def offset(p):
        if p % 2 == 0:
            return p
        return jnp.where(yl == 1, p, NH - p)

    def send_first_g():
        push(slab(yh), gb.at[0, 1], out_sem.at[1], g_rs.at[0], beside)
        push(slab(yh + 1 - 2 * yl), gb.at[0, 2], out_sem.at[1], g_rs.at[0], beside)

    def send_g(o):
        if o == 0:
            push(slab(yh), gb.at[1 + 2 * yl, 2], out_sem.at[1], g_rs.at[1 + 2 * yl], beyond)
        else:
            user = mod(yh - o, NH)
            push(slab(user), gb.at[o, 0], out_sem.at[1], g_own.at[o], {"yh": user})

    soon = 1 + 2 * yl
    late = 3 - 2 * yl

    def op_g(k):
        if k == 0:
            arrived(gb.at[soon, 0], g_own.at[soon])
            push(gb.at[soon, 0], gb.at[soon, 1], out_sem.at[1], g_rs.at[soon], beside)
        elif k == 1:
            arrived(gb.at[late, 0], g_own.at[late])
        elif k == 2:
            push(gb.at[soon, 0], gb.at[2, 2], out_sem.at[1], g_rs.at[2], beyond)
        elif k == 3:
            arrived(gb.at[2, 0], g_own.at[2])
            push(gb.at[2, 0], gb.at[2, 1], out_sem.at[1], g_rs.at[2], beside)
        else:
            push(gb.at[late, 0], gb.at[late, 1], out_sem.at[1], g_rs.at[late], beside)
            push(gb.at[2, 0], gb.at[3 - 2 * yl, 2], out_sem.at[1], g_rs.at[3 - 2 * yl], beyond)

    scale_load.wait()
    scales = sv[...].astype(F32).T.astype(BF)
    blocks = scales.shape[1]

    def dequant(b):
        pick = (lax.broadcasted_iota(jnp.int32, (blocks, HD), 0) == b).astype(F32).astype(BF)
        spread = jnp.dot(scales, pick, preferred_element_type=F32)
        v = xv[:, pl.ds(pl.multiple_of(b * HD, HD), HD)].astype(F32)
        return (v * spread).astype(BF)

    def prepare(i):
        xq = order_x(i)
        load(i).wait()

        @pl.loop(0, NZ, unroll=4)
        def _(zq):
            par, j = lax.rem(zq, 2), zq // 2
            s = lax.rem(zq + yl, 2)
            b = (xq * NZ + zq) * 2
            xs[xq * 8 + par * 4 + j] = dequant(b + 1 - s)
            xd[c, xq, par, j] = dequant(b + s)

    def share(i):
        xq = order_x(i)
        for par in range(2):
            s_out = lax.rem(par + yl + 1, 2)
            partner = {"yh": mod(yh + s_out * (2 * yl - 1), NH), "yl": 1 - yl}
            push(xs.at[pl.ds(xq * 8 + par * 4, 4)], xd.at[2 + c, xq, par], out_sem.at[0], xp_rs.at[xq, par], partner)

    def share_chip(i):
        xq = order_x(i)
        push(xd.at[c, xq], xd.at[c, xq], out_sem.at[0], xo_rs.at[xq], {"c": 1 - c})

    prepare(0)
    pl.semaphore_wait(barrier, len(x_line) + NZ - 1 + len(y_line))
    share(0)
    send_first_g()
    share_chip(0)

    @pl.loop(1, NX)
    def _(i):
        prepare(i)
        share(i)

    near = lax.rem(yl + 1, 2)

    def pass_on(i):
        xq = order_x(i)
        for k in range(2):
            par = lax.rem(near + k, 2)
            arrived(xd.at[2 + c, xq, par], xp_rs.at[xq, par])
            push(xd.at[2 + c, xq, par], xd.at[2 + c, xq, par], out_sem.at[0], xf_rs.at[xq], {"c": 1 - c})

    def product(p, i, xq):
        for par in range(2):
            s = lax.rem(par + yl, 2)
            lhs = jnp.concatenate([gt[0], gt[1 + s]], axis=1)
            for jj in range(2):
                rhs = jnp.concatenate(
                    [
                        jnp.concatenate([xd[k, xq, par, 2 * jj + e] for k in range(4)], axis=0)
                        for e in range(2)
                    ],
                    axis=1,
                )
                res = jnp.dot(lhs, rhs, preferred_element_type=F32).astype(BF)
                for e in range(2):
                    j = 2 * jj + e
                    wx[p][xq, par, j] = res[: ROWS[p], e * HD : (e + 1) * HD]
                    wz[p][2 * j + par, i] = res[ROWS[p] :, e * HD : (e + 1) * HD]

    def xdir(par):
        return 1 - 2 * par

    def after_product(p, i, xq):
        def when(k, run):
            if isinstance(i, int):
                if i == k:
                    run()
            else:
                pl.when(i == k)(run)

        def first():
            for par in range(2):
                d = xdir(par)
                push(wx[p].at[xq, par], rxl[p].at[par], rs_sem.at[p], xl_rs.at[p, par], {"x": mod(x + d, NX)})

        def second():
            push(wx[p].at[xq, 1], rxb[p].at[3], rs_sem.at[p], xb_rs.at[p], {"x": xq})

        def third():
            push(wx[p].at[xq, 0], rxb[p].at[2], rs_sem.at[p], xb_rs.at[p], {"x": xq})

        when(0, first)
        when(1, second)
        when(1, lambda: start_z(p, 0))
        when(2, third)
        when(3, lambda: start_z(p, 1))

    def start_z(p, h):
        z_long(p, 0, h)
        z_short(p, 0, h)

    def take_g(p):
        o = offset(p)
        if p == 0:
            own_g.wait()
        arrived(gb.at[o, pl.ds(1, 2)], g_rs.at[o])
        for k in range(3):
            gt[k] = gb[o, k].astype(F32).T.astype(BF)

    def op_m(p, i):
        if i == 0:
            pass_on(0)
            share_chip(1)
            take_g(0)
        xq = order_x(i)
        arrived(xd.at[1 - c, xq], xo_rs.at[xq])
        arrived(xd.at[3 - c, xq], xf_rs.at[xq])
        product(p, i, xq)
        after_product(p, i, xq)
        if i < NX - 1:
            pass_on(i + 1)
            if i < NX - 2:
                share_chip(i + 2)
        if i == 0:
            for o in (1, 3, 0):
                send_g(o)
        if i == 1:
            send_g(2)

    def op_n(p):
        take_g(p)

        @pl.loop(0, NX)
        def _(i):
            xq = order_x(i)
            product(p, i, xq)
            after_product(p, i, xq)

    def z_long(p, k, h):
        d = xdir(h)
        dst, rs = (rzf[p].at[h], zf_rs.at[p]) if k == 3 else (rzl[p].at[k, h], zl_rs.at[p, k, h])
        src = wz[p].at[mod(z + (4 - k) * d, NZ), pl.ds(2 * h, 2)]
        push(src, dst, rs_sem.at[p], rs, {"z": mod(z + d, NZ)})

    def z_short(p, k, h):
        d = xdir(h)
        dst, rs = (rzf[p].at[2 + h], zf_rs.at[p]) if k == 2 else (rzs[p].at[k, h], zs_rs.at[p, k, h])
        src = wz[p].at[mod(z - (3 - k) * d, NZ), pl.ds(2 * h, 2)]
        push(src, dst, rs_sem.at[p], rs, {"z": mod(z - d, NZ)})

    def z_long_add(p, k, h):
        t = mod(z + (3 - k) * xdir(h), NZ)
        arrived(rzl[p].at[k, h], zl_rs.at[p, k, h])
        for e in range(2):
            wz[p][t, 2 * h + e] = (wz[p][t, 2 * h + e].astype(F32) + rzl[p][k, h, e].astype(F32)).astype(BF)
        z_long(p, k + 1, h)

    def z_short_add(p, k, h):
        t = mod(z - (2 - k) * xdir(h), NZ)
        arrived(rzs[p].at[k, h], zs_rs.at[p, k, h])
        for e in range(2):
            wz[p][t, 2 * h + e] = (wz[p][t, 2 * h + e].astype(F32) + rzs[p][k, h, e].astype(F32)).astype(BF)
        z_short(p, k + 1, h)

    def pdir(p):
        return 1 - 2 * (p % 2)

    def z2_long(p, k, t):
        dst, rs = (f2z[p].at[0], fz_rs.at[p]) if k == 3 else (r2zl[p].at[k], z2l_rs.at[p, k])
        push(vb[p].at[t], dst, rs_sem.at[p], rs, {"z": mod(z + pdir(p), NZ)})

    def z2_short(p, k, t):
        dst, rs = (f2z[p].at[1], fz_rs.at[p]) if k == 2 else (r2zs[p].at[k], z2s_rs.at[p, k])
        push(vb[p].at[t], dst, rs_sem.at[p], rs, {"z": mod(z - pdir(p), NZ)})

    def z2_long_add(p, k):
        t = mod(z + (3 - k) * pdir(p), NZ)
        arrived(r2zl[p].at[k], z2l_rs.at[p, k])
        vb[p][t] = (vz[p][t] + r2zl[p][k].astype(F32)).astype(BF)
        z2_long(p, k + 1, t)

    def z2_short_add(p, k):
        t = mod(z - (2 - k) * pdir(p), NZ)
        arrived(r2zs[p].at[k], z2s_rs.at[p, k])
        vb[p][t] = (vz[p][t] + r2zs[p][k].astype(F32)).astype(BF)
        z2_short(p, k + 1, t)

    def op_xa(p, par):
        d = xdir(par)
        t = mod(x + d, NX)
        arrived(rxl[p].at[par], xl_rs.at[p, par])
        for j in range(4):
            wx[p][t, par, j] = (wx[p][t, par, j].astype(F32) + rxl[p][par, j].astype(F32)).astype(BF)
        push(wx[p].at[t, par], rxb[p].at[par], rs_sem.at[p], xb_rs.at[p], {"x": t})

    def op_xb(p):
        arrived(rxb[p], xb_rs.at[p])
        for par in range(2):
            for j in range(4):
                vz[p][2 * j + par] = (
                    wx[p][x, par, j].astype(F32) + rxb[p][2 + par, j].astype(F32) + rxb[p][par, j].astype(F32)
                )
        if p in TREE:
            start_tree(p)
            return
        d = pdir(p)
        t = mod(z + 4 * d, NZ)
        vb[p][t] = vz[p][t].astype(BF)
        z2_long(p, 0, t)
        t = mod(z - 3 * d, NZ)
        vb[p][t] = vz[p][t].astype(BF)
        z2_short(p, 0, t)

    def op_zb(p):
        arrived(rzf[p], zf_rs.at[p])
        for h in range(2):
            for e in range(2):
                uz[p][2 * h + e] = (
                    wz[p][z, 2 * h + e].astype(F32) + rzf[p][2 + h, e].astype(F32) + rzf[p][h, e].astype(F32)
                )
        d = pdir(p)
        ub[p][0] = uz[p][0].astype(BF)
        push(ub[p].at[0], r2x[p], rs_sem.at[p], x2_rs.at[p], {"x": mod(x + d, NX)})
        k = 2 - p % 2
        ub[p][k] = uz[p][k].astype(BF)
        push(ub[p].at[k], f2x[p].at[1], rs_sem.at[p], fx_rs.at[p], {"x": mod(x - d, NX)})

    def op_x2a(p):
        k = 1 + p % 2
        arrived(r2x[p], x2_rs.at[p])
        ub[p][k] = (uz[p][k] + r2x[p][...].astype(F32)).astype(BF)
        push(ub[p].at[k], f2x[p].at[0], rs_sem.at[p], fx_rs.at[p], {"x": mod(x + pdir(p), NX)})

    s_mine = lax.rem(z + yl, 2)
    stays = s_mine == yl

    def z_tree(p, k):
        d = pdir(p)
        if k == 0:
            t, got, rs, slot = mod(z + 3 * d, NZ), r2zl[p].at[0], z2l_rs.at[p, 0], 0
        elif k == 1:
            t, got, rs, slot = mod(z + d, NZ), r2zl[p].at[1], z2l_rs.at[p, 1], 1
        else:
            t, got, rs, slot = mod(z - 2 * d, NZ), r2zs[p].at[0], z2s_rs.at[p, 0], 2
        arrived(got, rs)
        vb[p][t] = (vz[p][t] + got[...].astype(F32)).astype(BF)
        push(vb[p].at[t], f2z[p].at[slot], rs_sem.at[p], fz_rs.at[p], {"z": t})

    def start_tree(p):
        d = pdir(p)
        near, back = {"z": mod(z + d, NZ)}, {"z": mod(z - d, NZ)}
        for steps, dst, rs, dev in (
            (4, r2zl[p].at[0], z2l_rs.at[p, 0], near),
            (-3, r2zs[p].at[0], z2s_rs.at[p, 0], back),
            (2, r2zl[p].at[1], z2l_rs.at[p, 1], near),
            (-1, f2z[p].at[3], fz_rs.at[p], back),
        ):
            t = mod(z + steps * d, NZ)
            vb[p][t] = vz[p][t].astype(BF)
            push(vb[p].at[t], dst, rs_sem.at[p], rs, dev)

    def give(p, first, rows):
        part = pl.ds(first, rows)
        far = 1 if p > 0 else 0

        def remote():
            o = offset(p)
            dev = {"yh": mod(yh + o, NH), "yl": s_mine}
            push(ty.at[p, part], ry.at[o, part], out_sem.at[2 + far], y_rs.at[far], dev)

        if p > 0:
            remote()
        else:
            pl.when(jnp.logical_not(stays))(remote)

            @pl.when(stays)
            def _():
                ry[0, part] = ty[0, part]

    def op_fx(p):
        arrived(f2x[p], fx_rs.at[p])
        ty[p, ROWS[p] :] = uz[p][3] + f2x[p][0].astype(F32) + f2x[p][1].astype(F32)
        give(p, ROWS[p], HD - ROWS[p])

    def op_fz(p):
        arrived(f2z[p], fz_rs.at[p])
        total = vz[p][z]
        for k in range(f2z[p].shape[0]):
            total += f2z[p][k].astype(F32)
        ty[p, : ROWS[p]] = total
        give(p, 0, ROWS[p])

    ops = {
        "G": op_g, "M": op_m, "N": op_n, "xa": op_xa, "xb": op_xb, "zl": z_long_add, "zs": z_short_add,
        "z2l": z2_long_add, "z2s": z2_short_add, "zb": op_zb, "x2a": op_x2a, "fx": op_fx, "fz": op_fz, "zt": z_tree,
    }

    for name, *where in SEQUENCE:
        ops[name](*where)

    sent(xd.at[pl.ds(0, 3)], out_sem.at[0])
    sent(xs.at[pl.ds(0, 22)], out_sem.at[1])
    for p in range(PHASES):
        sent(xs.at[pl.ds(0, 31)], rs_sem.at[p])
    arrived(ry.at[pl.ds(1, PHASES - 1)], y_rs.at[1])

    @pl.when(jnp.logical_not(stays))
    def _():
        arrived(ry.at[0], y_rs.at[0])

    total = ry[0] + ry[1] + ry[2] + ry[3]
    part = jnp.sum(total * total, axis=0, keepdims=True)

    def spot(k, e):
        return mod(x + k, NX) * NC + mod(c + e, NC)

    nsrc[0] = part
    for k, e in x_line:
        push(nsrc.at[0], n1.at[spot(0, 0)], out_sem.at[4], n_rs.at[0], x_dev(k, e))
    n1[spot(0, 0)] = part
    out_ref[...] = total.T
    arrived(n1.at[pl.ds(0, len(x_line))], n_rs.at[0])
    part = jnp.sum(n1[...], axis=0)

    nsrc[1] = part
    for k in range(1, NZ):
        t = mod(z + k, NZ)
        push(nsrc.at[1], n2.at[z], out_sem.at[5], n_rs.at[1], {"z": t})
    n2[z] = part
    sent(n1.at[pl.ds(0, len(x_line))], out_sem.at[4])
    arrived(n2.at[pl.ds(0, NZ - 1)], n_rs.at[1])
    part = jnp.sum(n2[...], axis=0)

    def place(a, b):
        return mod(yh + a, NH) * NL + mod(yl + b, NL)

    nsrc[2] = part
    for a, b in y_line:
        push(nsrc.at[2], n3.at[place(0, 0)], out_sem.at[6], n_rs.at[2], y_dev(a, b))
    n3[place(0, 0)] = part
    sent(n2.at[pl.ds(0, NZ - 1)], out_sem.at[5])

    @pl.when(jnp.logical_not(stays))
    def _():
        sent(ty.at[0], out_sem.at[2])

    sent(ty.at[pl.ds(1, PHASES - 1)], out_sem.at[3])
    arrived(n3.at[pl.ds(0, len(y_line))], n_rs.at[2])
    part = jnp.sum(n3[...], axis=0)
    whole = jnp.sum(part, axis=1, keepdims=True)
    out_ref[...] = out_ref[...] * jnp.minimum(jnp.float32(1.0), jnp.float32(limit) / jnp.sqrt(whole))
    sent(n3.at[pl.ds(0, len(y_line))], out_sem.at[6])


def phase_scratch(rx, rz, last):
    shapes = [
        (NX, 2, 4, rx), (NZ, NX, rz), (2, 4, rx), (4, 4, rx), (3, 2, 2, rz), (2, 2, 2, rz), (4, 2, rz),
        (NZ, rx), (NZ, rx), (NX, rz), (NX, rz), (3, rx), (2, rx), (rz,), (last, rx), (2, rz),
    ]
    return [pltpu.VMEM((*s, HD), F32 if k in (7, 9) else BF) for k, s in enumerate(shapes)]


def body(stash_values, stash_scales, value_grad):
    tokens, width = stash_values.shape
    limit = math.sqrt(width * HD * lax.axis_size("yh") * lax.axis_size("c"))
    dma = pltpu.SemaphoreType.DMA
    return pl.pallas_call(
        functools.partial(kernel, limit),
        out_shape=jax.ShapeDtypeStruct((HD, HD), F32),
        in_specs=[
            pl.BlockSpec(memory_space=pl.ANY),
            pl.BlockSpec(memory_space=pl.ANY),
            pl.BlockSpec(memory_space=pl.ANY),
        ],
        out_specs=pl.BlockSpec(memory_space=pltpu.VMEM),
        scratch_shapes=[
            pltpu.VMEM((tokens, width), BF),
            pltpu.VMEM((stash_scales.shape[1], tokens), BF),
            pltpu.VMEM((4, NX, 2, 4, TOK, HD), BF),
            pltpu.VMEM((NX * 8, TOK, HD), BF),
            pltpu.VMEM((NH, 3, 2 * TOK, HD), BF),
            pltpu.VMEM((3, HD, 2 * TOK), BF),
            pltpu.VMEM((PHASES, HD, HD), F32),
            pltpu.VMEM((PHASES, HD, HD), F32),
            pltpu.VMEM((3, 1, HD), F32),
            pltpu.VMEM((NX * NC, 1, HD), F32),
            pltpu.VMEM((NZ, 1, HD), F32),
            pltpu.VMEM((NH * NL, 1, HD), F32),
            dma((NX + 2,)),
            dma((7,)),
            dma((PHASES,)),
            dma((NH,)),
            dma((NH,)),
            dma((NX,)),
            dma((NX, 2)),
            dma((NX,)),
            dma((PHASES, 2)),
            dma((PHASES,)),
            dma((PHASES, 3, 2)),
            dma((PHASES, 2, 2)),
            dma((PHASES,)),
            dma((PHASES, 3)),
            dma((PHASES, 2)),
            dma((PHASES,)),
            dma((PHASES,)),
            dma((PHASES,)),
            dma((2,)),
            dma((3,)),
            *(ref for p, rows in enumerate(ROWS) for ref in phase_scratch(rows, HD - rows, 4 if p in TREE else 2)),
        ],
        compiler_params=pltpu.CompilerParams(
            collective_id=0, has_side_effects=True, vmem_limit_bytes=56 * 1024 * 1024
        ),
    )(stash_values, stash_scales.T, value_grad)


def solution(mesh):
    torus = Mesh(mesh.devices.reshape(NX, NZ, NL, NH, NC), AXES)
    rows = ("x", "z", "yl", "yh", "c")
    return jax.shard_map(
        body,
        mesh=torus,
        in_specs=(P(rows, None), P(rows, None), P(("x", "z", "yl"), ("yh", "c"))),
        out_specs=P(("x", "z", "yl"), ("yh", "c")),
        check_vma=False,
    )
```

```python
import functools
import math

import jax
import jax.numpy as jnp
from jax import lax
from jax.experimental import pallas as pl
from jax.experimental.pallas import tpu as pltpu
from jax.sharding import Mesh
from jax.sharding import PartitionSpec as P

MESH = pl.DeviceIdType.MESH
NX, NZ, NH, NL, NC = 4, 8, 4, 2, 2
AXES = ("x", "z", "yl", "yh", "c")
HD = 128
TOK = 128
ROWS = (80, 80, 80, 80)
PHASES = NH
TREE = (2, 3)
SEQUENCE = (
    ("M", 0, 0), ("M", 0, 1), ("xa", 0, 0), ("M", 0, 2), ("G", 0), ("xa", 0, 1), ("M", 0, 3), ("G", 1), ("G", 2),
    ("zl", 0, 0, 0), ("zs", 0, 0, 0), ("G", 3), ("N", 1), ("G", 4), ("xb", 0), ("zl", 0, 1, 0), ("zs", 0, 1, 0),
    ("zl", 0, 0, 1), ("zs", 0, 0, 1), ("N", 2), ("z2l", 0, 0), ("z2s", 0, 0), ("zl", 0, 2, 0), ("xa", 1, 0),
    ("xa", 1, 1), ("zl", 0, 1, 1), ("zs", 0, 1, 1), ("zl", 1, 0, 0), ("zs", 1, 0, 0), ("zl", 1, 0, 1),
    ("zs", 1, 0, 1), ("N", 3), ("zl", 2, 0, 0), ("z2l", 0, 1), ("z2s", 0, 1), ("xa", 2, 0), ("xa", 2, 1),
    ("zs", 2, 0, 0), ("zl", 0, 2, 1), ("zl", 2, 0, 1), ("zs", 2, 0, 1), ("zs", 1, 1, 0), ("zl", 1, 1, 0),
    ("zl", 1, 1, 1), ("zs", 1, 1, 1), ("zs", 3, 0, 0), ("zl", 3, 0, 0), ("zl", 3, 0, 1), ("zs", 3, 0, 1),
    ("zs", 2, 1, 0), ("zl", 2, 1, 0), ("xb", 1), ("z2l", 0, 2), ("zb", 0), ("zs", 2, 1, 1), ("zl", 2, 1, 1),
    ("zl", 1, 2, 0), ("xa", 3, 0), ("xa", 3, 1), ("zl", 1, 2, 1), ("zl", 3, 1, 0), ("zs", 3, 1, 0), ("zs", 3, 1, 1),
    ("zl", 3, 1, 1), ("zl", 2, 2, 0), ("z2s", 1, 0), ("z2l", 1, 0), ("fz", 0), ("zl", 2, 2, 1), ("xb", 2),
    ("x2a", 0), ("zb", 1), ("zl", 3, 2, 0), ("zl", 3, 2, 1), ("z2l", 1, 1), ("zb", 2), ("xb", 3), ("fx", 0),
    ("x2a", 1), ("z2s", 1, 1), ("zt", 2, 0), ("zt", 2, 2), ("zt", 2, 1), ("zb", 3), ("z2l", 1, 2), ("x2a", 2),
    ("zt", 3, 0), ("zt", 3, 2), ("fx", 1), ("zt", 3, 1), ("x2a", 3), ("fx", 2), ("fz", 1), ("fz", 2), ("fx", 3),
    ("fz", 3),
)
BF = jnp.bfloat16
F32 = jnp.float32


def mod(value, n):
    return lax.rem(value + 4 * n, n)


def kernel(
    limit, x_hbm, s_hbm, g_hbm, out_ref, *scratch
):
    x, z, yl, yh, c = (lax.axis_index(name) for name in AXES)
    quarter = NZ * 2 * HD
    xv, sv, xd, xs, gb, gt, ty, ry, nsrc, n1, n2, n3 = scratch[:12]
    (
        ld_sem, out_sem, rs_sem, g_own, g_rs, xo_rs, xp_rs, xf_rs,
        xl_rs, xb_rs, zl_rs, zs_rs, zf_rs, z2l_rs, z2s_rs, x2_rs, fz_rs, fx_rs,
        y_rs, n_rs,
    ) = scratch[12:32]
    (
        wx, wz, rxl, rxb, rzl, rzs, rzf, vz, vb, uz, ub, r2zl, r2zs, r2x, f2z, f2x,
    ) = (scratch[32 + k :: 16] for k in range(16))

    def push(src, dst, ss, rs, dev):
        pltpu.make_async_remote_copy(
            src_ref=src, dst_ref=dst, send_sem=ss, recv_sem=rs, device_id=dev, device_id_type=MESH
        ).start()

    def arrived(dst, rs):
        pltpu.make_async_remote_copy(
            src_ref=dst, dst_ref=dst, send_sem=rs, recv_sem=rs, device_id={"c": 1 - c}, device_id_type=MESH
        ).wait_recv()

    def sent(src, ss):
        pltpu.make_async_remote_copy(
            src_ref=src, dst_ref=src, send_sem=ss, recv_sem=ss, device_id={"c": 1 - c}, device_id_type=MESH
        ).wait_send()

    def order_x(i):
        if isinstance(i, int):
            return mod(x + (2, 1, 3, 0)[i], NX)
        return mod(x + jnp.where(i == 0, 2, jnp.where(i == 1, 1, jnp.where(i == 2, 3, 0))), NX)

    def load(i):
        xq = order_x(i)
        cols = pl.ds(pl.multiple_of(xq * quarter, quarter), quarter)
        return pltpu.make_async_copy(x_hbm.at[:, cols], xv.at[:, cols], ld_sem.at[i])

    load(0).start()
    own_g = pltpu.make_async_copy(g_hbm.at[pl.ds(pl.multiple_of(yh * 256, 256), 256), :], gb.at[0, 0], ld_sem.at[NX])
    scale_load = pltpu.make_async_copy(s_hbm, sv, ld_sem.at[NX + 1])
    scale_load.start()

    barrier = pltpu.get_barrier_semaphore()

    def greet(dev):
        pl.semaphore_signal(barrier, inc=1, device_id=dev, device_id_type=MESH)

    plane = [(k, e, w) for k in range(NX) for e in range(NC) for w in range(NZ) if (k, e, w) != (0, 0, 0)]
    y_line = [(a, b) for a in range(NH) for b in range(NL) if (a, b) != (0, 0)]

    def plane_dev(k, e, w):
        return {"x": mod(x + k, NX), "c": mod(c + e, NC), "z": mod(z + w, NZ)}

    def y_dev(a, b):
        return {"yh": mod(yh + a, NH), "yl": mod(yl + b, NL)}

    met = [step for step in plane if step[2] == 0 or step[:2] == (0, 0)]
    for step in met:
        greet(plane_dev(*step))
    for a, b in y_line:
        greet(y_dev(a, b))

    for i in range(1, NX):
        load(i).start()
    own_g.start()

    def slab(k):
        return g_hbm.at[pl.ds(pl.multiple_of(mod(k, NH) * 256, 256), 256), :]

    beside = {"yl": 1 - yl}
    beyond = {"yh": mod(yh + 2 * yl - 1, NH), "yl": 1 - yl}

    def offset(p):
        if p % 2 == 0:
            return p
        return jnp.where(yl == 1, p, NH - p)

    def send_first_g():
        push(slab(yh), gb.at[0, 1], out_sem.at[1], g_rs.at[0], beside)
        push(slab(yh + 1 - 2 * yl), gb.at[0, 2], out_sem.at[1], g_rs.at[0], beside)

    def send_g(o):
        if o == 0:
            push(slab(yh), gb.at[1 + 2 * yl, 2], out_sem.at[1], g_rs.at[1 + 2 * yl], beyond)
        else:
            user = mod(yh - o, NH)
            push(slab(user), gb.at[o, 0], out_sem.at[1], g_own.at[o], {"yh": user})

    soon = 1 + 2 * yl
    late = 3 - 2 * yl

    def op_g(k):
        if k == 0:
            arrived(gb.at[soon, 0], g_own.at[soon])
            push(gb.at[soon, 0], gb.at[soon, 1], out_sem.at[1], g_rs.at[soon], beside)
        elif k == 1:
            arrived(gb.at[late, 0], g_own.at[late])
        elif k == 2:
            push(gb.at[soon, 0], gb.at[2, 2], out_sem.at[1], g_rs.at[2], beyond)
        elif k == 3:
            arrived(gb.at[2, 0], g_own.at[2])
            push(gb.at[2, 0], gb.at[2, 1], out_sem.at[1], g_rs.at[2], beside)
        else:
            push(gb.at[late, 0], gb.at[late, 1], out_sem.at[1], g_rs.at[late], beside)
            push(gb.at[2, 0], gb.at[3 - 2 * yl, 2], out_sem.at[1], g_rs.at[3 - 2 * yl], beyond)

    scale_load.wait()
    scales = sv[...].astype(F32).T.astype(BF)
    blocks = scales.shape[1]

    def dequant(b):
        pick = (lax.broadcasted_iota(jnp.int32, (blocks, HD), 0) == b).astype(F32).astype(BF)
        spread = jnp.dot(scales, pick, preferred_element_type=F32)
        v = xv[:, pl.ds(pl.multiple_of(b * HD, HD), HD)].astype(F32)
        return (v * spread).astype(BF)

    def prepare(i):
        xq = order_x(i)
        load(i).wait()

        @pl.loop(0, NZ, unroll=4)
        def _(zq):
            par, j = lax.rem(zq, 2), zq // 2
            s = lax.rem(zq + yl, 2)
            b = (xq * NZ + zq) * 2
            xs[xq * 8 + par * 4 + j] = dequant(b + 1 - s)
            xd[c, xq, par, j] = dequant(b + s)

    def share(i):
        xq = order_x(i)
        for par in range(2):
            s_out = lax.rem(par + yl + 1, 2)
            partner = {"yh": mod(yh + s_out * (2 * yl - 1), NH), "yl": 1 - yl}
            push(xs.at[pl.ds(xq * 8 + par * 4, 4)], xd.at[2 + c, xq, par], out_sem.at[0], xp_rs.at[xq, par], partner)

    def share_chip(i):
        xq = order_x(i)
        push(xd.at[c, xq], xd.at[c, xq], out_sem.at[0], xo_rs.at[xq], {"c": 1 - c})

    prepare(0)
    pl.semaphore_wait(barrier, len(met) + len(y_line))
    share(0)
    send_first_g()
    share_chip(0)

    @pl.loop(1, NX)
    def _(i):
        prepare(i)
        share(i)

    near = lax.rem(yl + 1, 2)

    def pass_on(i):
        xq = order_x(i)
        for k in range(2):
            par = lax.rem(near + k, 2)
            arrived(xd.at[2 + c, xq, par], xp_rs.at[xq, par])
            push(xd.at[2 + c, xq, par], xd.at[2 + c, xq, par], out_sem.at[0], xf_rs.at[xq], {"c": 1 - c})

    def product(p, i, xq):
        for par in range(2):
            s = lax.rem(par + yl, 2)
            lhs = jnp.concatenate([gt[0], gt[1 + s]], axis=1)
            for jj in range(2):
                rhs = jnp.concatenate(
                    [
                        jnp.concatenate([xd[k, xq, par, 2 * jj + e] for k in range(4)], axis=0)
                        for e in range(2)
                    ],
                    axis=1,
                )
                res = jnp.dot(lhs, rhs, preferred_element_type=F32).astype(BF)
                for e in range(2):
                    j = 2 * jj + e
                    wx[p][xq, par, j] = res[: ROWS[p], e * HD : (e + 1) * HD]
                    wz[p][2 * j + par, i] = res[ROWS[p] :, e * HD : (e + 1) * HD]

    def xdir(par):
        return 1 - 2 * par

    def after_product(p, i, xq):
        def when(k, run):
            if isinstance(i, int):
                if i == k:
                    run()
            else:
                pl.when(i == k)(run)

        def first():
            for par in range(2):
                d = xdir(par)
                push(wx[p].at[xq, par], rxl[p].at[par], rs_sem.at[p], xl_rs.at[p, par], {"x": mod(x + d, NX)})

        def second():
            push(wx[p].at[xq, 1], rxb[p].at[3], rs_sem.at[p], xb_rs.at[p], {"x": xq})

        def third():
            push(wx[p].at[xq, 0], rxb[p].at[2], rs_sem.at[p], xb_rs.at[p], {"x": xq})

        when(0, first)
        when(1, second)
        when(1, lambda: start_z(p, 0))
        when(2, third)
        when(3, lambda: start_z(p, 1))

    def start_z(p, h):
        z_long(p, 0, h)
        z_short(p, 0, h)

    def take_g(p):
        o = offset(p)
        if p == 0:
            own_g.wait()
        arrived(gb.at[o, pl.ds(1, 2)], g_rs.at[o])
        for k in range(3):
            gt[k] = gb[o, k].astype(F32).T.astype(BF)

    def op_m(p, i):
        if i == 0:
            pass_on(0)
            share_chip(1)
            take_g(0)
        xq = order_x(i)
        arrived(xd.at[1 - c, xq], xo_rs.at[xq])
        arrived(xd.at[3 - c, xq], xf_rs.at[xq])
        product(p, i, xq)
        after_product(p, i, xq)
        if i < NX - 1:
            pass_on(i + 1)
            if i < NX - 2:
                share_chip(i + 2)
        if i == 0:
            for o in (1, 3, 0):
                send_g(o)
        if i == 1:
            send_g(2)

    def op_n(p):
        take_g(p)

        @pl.loop(0, NX)
        def _(i):
            xq = order_x(i)
            product(p, i, xq)
            after_product(p, i, xq)

    def z_long(p, k, h):
        d = xdir(h)
        dst, rs = (rzf[p].at[h], zf_rs.at[p]) if k == 3 else (rzl[p].at[k, h], zl_rs.at[p, k, h])
        src = wz[p].at[mod(z + (4 - k) * d, NZ), pl.ds(2 * h, 2)]
        push(src, dst, rs_sem.at[p], rs, {"z": mod(z + d, NZ)})

    def z_short(p, k, h):
        d = xdir(h)
        dst, rs = (rzf[p].at[2 + h], zf_rs.at[p]) if k == 2 else (rzs[p].at[k, h], zs_rs.at[p, k, h])
        src = wz[p].at[mod(z - (3 - k) * d, NZ), pl.ds(2 * h, 2)]
        push(src, dst, rs_sem.at[p], rs, {"z": mod(z - d, NZ)})

    def z_long_add(p, k, h):
        t = mod(z + (3 - k) * xdir(h), NZ)
        arrived(rzl[p].at[k, h], zl_rs.at[p, k, h])
        for e in range(2):
            wz[p][t, 2 * h + e] = (wz[p][t, 2 * h + e].astype(F32) + rzl[p][k, h, e].astype(F32)).astype(BF)
        z_long(p, k + 1, h)

    def z_short_add(p, k, h):
        t = mod(z - (2 - k) * xdir(h), NZ)
        arrived(rzs[p].at[k, h], zs_rs.at[p, k, h])
        for e in range(2):
            wz[p][t, 2 * h + e] = (wz[p][t, 2 * h + e].astype(F32) + rzs[p][k, h, e].astype(F32)).astype(BF)
        z_short(p, k + 1, h)

    def pdir(p):
        return 1 - 2 * (p % 2)

    def z2_long(p, k, t):
        dst, rs = (f2z[p].at[0], fz_rs.at[p]) if k == 3 else (r2zl[p].at[k], z2l_rs.at[p, k])
        push(vb[p].at[t], dst, rs_sem.at[p], rs, {"z": mod(z + pdir(p), NZ)})

    def z2_short(p, k, t):
        dst, rs = (f2z[p].at[1], fz_rs.at[p]) if k == 2 else (r2zs[p].at[k], z2s_rs.at[p, k])
        push(vb[p].at[t], dst, rs_sem.at[p], rs, {"z": mod(z - pdir(p), NZ)})

    def z2_long_add(p, k):
        t = mod(z + (3 - k) * pdir(p), NZ)
        arrived(r2zl[p].at[k], z2l_rs.at[p, k])
        vb[p][t] = (vz[p][t] + r2zl[p][k].astype(F32)).astype(BF)
        z2_long(p, k + 1, t)

    def z2_short_add(p, k):
        t = mod(z - (2 - k) * pdir(p), NZ)
        arrived(r2zs[p].at[k], z2s_rs.at[p, k])
        vb[p][t] = (vz[p][t] + r2zs[p][k].astype(F32)).astype(BF)
        z2_short(p, k + 1, t)

    def op_xa(p, par):
        d = xdir(par)
        t = mod(x + d, NX)
        arrived(rxl[p].at[par], xl_rs.at[p, par])
        for j in range(4):
            wx[p][t, par, j] = (wx[p][t, par, j].astype(F32) + rxl[p][par, j].astype(F32)).astype(BF)
        push(wx[p].at[t, par], rxb[p].at[par], rs_sem.at[p], xb_rs.at[p], {"x": t})

    def op_xb(p):
        arrived(rxb[p], xb_rs.at[p])
        for par in range(2):
            for j in range(4):
                vz[p][2 * j + par] = (
                    wx[p][x, par, j].astype(F32) + rxb[p][2 + par, j].astype(F32) + rxb[p][par, j].astype(F32)
                )
        if p in TREE:
            start_tree(p)
            return
        d = pdir(p)
        t = mod(z + 4 * d, NZ)
        vb[p][t] = vz[p][t].astype(BF)
        z2_long(p, 0, t)
        t = mod(z - 3 * d, NZ)
        vb[p][t] = vz[p][t].astype(BF)
        z2_short(p, 0, t)

    def op_zb(p):
        arrived(rzf[p], zf_rs.at[p])
        for h in range(2):
            for e in range(2):
                uz[p][2 * h + e] = (
                    wz[p][z, 2 * h + e].astype(F32) + rzf[p][2 + h, e].astype(F32) + rzf[p][h, e].astype(F32)
                )
        d = pdir(p)
        ub[p][0] = uz[p][0].astype(BF)
        push(ub[p].at[0], r2x[p], rs_sem.at[p], x2_rs.at[p], {"x": mod(x + d, NX)})
        k = 2 - p % 2
        ub[p][k] = uz[p][k].astype(BF)
        push(ub[p].at[k], f2x[p].at[1], rs_sem.at[p], fx_rs.at[p], {"x": mod(x - d, NX)})

    def op_x2a(p):
        k = 1 + p % 2
        arrived(r2x[p], x2_rs.at[p])
        ub[p][k] = (uz[p][k] + r2x[p][...].astype(F32)).astype(BF)
        push(ub[p].at[k], f2x[p].at[0], rs_sem.at[p], fx_rs.at[p], {"x": mod(x + pdir(p), NX)})

    s_mine = lax.rem(z + yl, 2)
    stays = s_mine == yl

    def z_tree(p, k):
        d = pdir(p)
        if k == 0:
            t, got, rs, slot = mod(z + 3 * d, NZ), r2zl[p].at[0], z2l_rs.at[p, 0], 0
        elif k == 1:
            t, got, rs, slot = mod(z + d, NZ), r2zl[p].at[1], z2l_rs.at[p, 1], 1
        else:
            t, got, rs, slot = mod(z - 2 * d, NZ), r2zs[p].at[0], z2s_rs.at[p, 0], 2
        arrived(got, rs)
        vb[p][t] = (vz[p][t] + got[...].astype(F32)).astype(BF)
        push(vb[p].at[t], f2z[p].at[slot], rs_sem.at[p], fz_rs.at[p], {"z": t})

    def start_tree(p):
        d = pdir(p)
        near, back = {"z": mod(z + d, NZ)}, {"z": mod(z - d, NZ)}
        for steps, dst, rs, dev in (
            (4, r2zl[p].at[0], z2l_rs.at[p, 0], near),
            (-3, r2zs[p].at[0], z2s_rs.at[p, 0], back),
            (2, r2zl[p].at[1], z2l_rs.at[p, 1], near),
            (-1, f2z[p].at[3], fz_rs.at[p], back),
        ):
            t = mod(z + steps * d, NZ)
            vb[p][t] = vz[p][t].astype(BF)
            push(vb[p].at[t], dst, rs_sem.at[p], rs, dev)

    def give(p, first, rows):
        part = pl.ds(first, rows)
        far = 1 if p > 0 else 0

        def remote():
            o = offset(p)
            dev = {"yh": mod(yh + o, NH), "yl": s_mine}
            push(ty.at[p, part], ry.at[o, part], out_sem.at[2 + far], y_rs.at[far], dev)

        if p > 0:
            remote()
        else:
            pl.when(jnp.logical_not(stays))(remote)

            @pl.when(stays)
            def _():
                ry[0, part] = ty[0, part]

    def op_fx(p):
        arrived(f2x[p], fx_rs.at[p])
        ty[p, ROWS[p] :] = uz[p][3] + f2x[p][0].astype(F32) + f2x[p][1].astype(F32)
        give(p, ROWS[p], HD - ROWS[p])

    def op_fz(p):
        arrived(f2z[p], fz_rs.at[p])
        total = vz[p][z]
        for k in range(f2z[p].shape[0]):
            total += f2z[p][k].astype(F32)
        ty[p, : ROWS[p]] = total
        give(p, 0, ROWS[p])

    ops = {
        "G": op_g, "M": op_m, "N": op_n, "xa": op_xa, "xb": op_xb, "zl": z_long_add, "zs": z_short_add,
        "z2l": z2_long_add, "z2s": z2_short_add, "zb": op_zb, "x2a": op_x2a, "fx": op_fx, "fz": op_fz, "zt": z_tree,
    }

    for name, *where in SEQUENCE:
        ops[name](*where)

    sent(xd.at[pl.ds(0, 3)], out_sem.at[0])
    sent(xs.at[pl.ds(0, 22)], out_sem.at[1])
    for p in range(PHASES):
        sent(xs.at[pl.ds(0, 31)], rs_sem.at[p])
    arrived(ry.at[pl.ds(1, PHASES - 1)], y_rs.at[1])

    @pl.when(jnp.logical_not(stays))
    def _():
        arrived(ry.at[0], y_rs.at[0])

    total = ry[0] + ry[1] + ry[2] + ry[3]
    part = jnp.sum(total * total, axis=0, keepdims=True)

    def spot(k, e, w):
        return (mod(x + k, NX) * NC + mod(c + e, NC)) * NZ + mod(z + w, NZ)

    mine = spot(0, 0, 0)
    nsrc[0] = part
    for step in plane:
        push(nsrc.at[0], n1.at[mine], out_sem.at[4], n_rs.at[0], plane_dev(*step))
    n1[mine] = part
    out_ref[...] = total.T
    arrived(n1.at[pl.ds(0, len(plane))], n_rs.at[0])
    part = jnp.sum(n1[...], axis=0)

    def place(a, b):
        return mod(yh + a, NH) * NL + mod(yl + b, NL)

    nsrc[2] = part
    for a, b in y_line:
        push(nsrc.at[2], n3.at[place(0, 0)], out_sem.at[6], n_rs.at[2], y_dev(a, b))
    n3[place(0, 0)] = part
    sent(n1.at[pl.ds(0, len(plane))], out_sem.at[4])

    @pl.when(jnp.logical_not(stays))
    def _():
        sent(ty.at[0], out_sem.at[2])

    sent(ty.at[pl.ds(1, PHASES - 1)], out_sem.at[3])
    arrived(n3.at[pl.ds(0, len(y_line))], n_rs.at[2])
    part = jnp.sum(n3[...], axis=0)
    whole = jnp.sum(part, axis=1, keepdims=True)
    out_ref[...] = out_ref[...] * jnp.minimum(jnp.float32(1.0), jnp.float32(limit) / jnp.sqrt(whole))
    sent(n3.at[pl.ds(0, len(y_line))], out_sem.at[6])


def phase_scratch(rx, rz, last):
    shapes = [
        (NX, 2, 4, rx), (NZ, NX, rz), (2, 4, rx), (4, 4, rx), (3, 2, 2, rz), (2, 2, 2, rz), (4, 2, rz),
        (NZ, rx), (NZ, rx), (NX, rz), (NX, rz), (3, rx), (2, rx), (rz,), (last, rx), (2, rz),
    ]
    return [pltpu.VMEM((*s, HD), F32 if k in (7, 9) else BF) for k, s in enumerate(shapes)]


def body(stash_values, stash_scales, value_grad):
    tokens, width = stash_values.shape
    limit = math.sqrt(width * HD * lax.axis_size("yh") * lax.axis_size("c"))
    dma = pltpu.SemaphoreType.DMA
    return pl.pallas_call(
        functools.partial(kernel, limit),
        out_shape=jax.ShapeDtypeStruct((HD, HD), F32),
        in_specs=[
            pl.BlockSpec(memory_space=pl.ANY),
            pl.BlockSpec(memory_space=pl.ANY),
            pl.BlockSpec(memory_space=pl.ANY),
        ],
        out_specs=pl.BlockSpec(memory_space=pltpu.VMEM),
        scratch_shapes=[
            pltpu.VMEM((tokens, width), BF),
            pltpu.VMEM((stash_scales.shape[1], tokens), BF),
            pltpu.VMEM((4, NX, 2, 4, TOK, HD), BF),
            pltpu.VMEM((NX * 8, TOK, HD), BF),
            pltpu.VMEM((NH, 3, 2 * TOK, HD), BF),
            pltpu.VMEM((3, HD, 2 * TOK), BF),
            pltpu.VMEM((PHASES, HD, HD), F32),
            pltpu.VMEM((PHASES, HD, HD), F32),
            pltpu.VMEM((3, 1, HD), F32),
            pltpu.VMEM((NX * NC * NZ, 1, HD), F32),
            pltpu.VMEM((NZ, 1, HD), F32),
            pltpu.VMEM((NH * NL, 1, HD), F32),
            dma((NX + 2,)),
            dma((7,)),
            dma((PHASES,)),
            dma((NH,)),
            dma((NH,)),
            dma((NX,)),
            dma((NX, 2)),
            dma((NX,)),
            dma((PHASES, 2)),
            dma((PHASES,)),
            dma((PHASES, 3, 2)),
            dma((PHASES, 2, 2)),
            dma((PHASES,)),
            dma((PHASES, 3)),
            dma((PHASES, 2)),
            dma((PHASES,)),
            dma((PHASES,)),
            dma((PHASES,)),
            dma((2,)),
            dma((3,)),
            *(ref for p, rows in enumerate(ROWS) for ref in phase_scratch(rows, HD - rows, 4 if p in TREE else 2)),
        ],
        compiler_params=pltpu.CompilerParams(
            collective_id=0, has_side_effects=True, vmem_limit_bytes=56 * 1024 * 1024
        ),
    )(stash_values, stash_scales.T, value_grad)


def solution(mesh):
    torus = Mesh(mesh.devices.reshape(NX, NZ, NL, NH, NC), AXES)
    rows = ("x", "z", "yl", "yh", "c")
    return jax.shard_map(
        body,
        mesh=torus,
        in_specs=(P(rows, None), P(rows, None), P(("x", "z", "yl"), ("yh", "c"))),
        out_specs=P(("x", "z", "yl"), ("yh", "c")),
        check_vma=False,
    )
```

```python
import functools
import math

import jax
import jax.numpy as jnp
from jax import lax
from jax.experimental import pallas as pl
from jax.experimental.pallas import tpu as pltpu
from jax.sharding import Mesh
from jax.sharding import PartitionSpec as P

MESH = pl.DeviceIdType.MESH
NX, NZ, NH, NL, NC = 4, 8, 4, 2, 2
AXES = ("x", "z", "yl", "yh", "c")
HD = 128
TOK = 128
ROWS = (80, 80, 80, 80)
PHASES = NH
TREE = (2, 3)
SEQUENCE = (
    ("M", 0, 0), ("M", 0, 1), ("xa", 0, 0), ("M", 0, 2), ("G", 0), ("xa", 0, 1), ("M", 0, 3), ("G", 1), ("G", 2),
    ("zl", 0, 0, 0), ("zs", 0, 0, 0), ("G", 3), ("N", 1), ("G", 4), ("xb", 0), ("zl", 0, 1, 0), ("zs", 0, 1, 0),
    ("zl", 0, 0, 1), ("zs", 0, 0, 1), ("N", 2), ("z2l", 0, 0), ("z2s", 0, 0), ("zl", 0, 2, 0), ("xa", 1, 0),
    ("xa", 1, 1), ("zl", 0, 1, 1), ("zs", 0, 1, 1), ("zl", 1, 0, 0), ("zs", 1, 0, 0), ("zl", 1, 0, 1),
    ("zs", 1, 0, 1), ("N", 3), ("zl", 2, 0, 0), ("z2l", 0, 1), ("z2s", 0, 1), ("xa", 2, 0), ("xa", 2, 1),
    ("zs", 2, 0, 0), ("zl", 0, 2, 1), ("zl", 2, 0, 1), ("zs", 2, 0, 1), ("zs", 1, 1, 0), ("zl", 1, 1, 0),
    ("zl", 1, 1, 1), ("zs", 1, 1, 1), ("zs", 3, 0, 0), ("zl", 3, 0, 0), ("zl", 3, 0, 1), ("zs", 3, 0, 1),
    ("zs", 2, 1, 0), ("zl", 2, 1, 0), ("xb", 1), ("z2l", 0, 2), ("zb", 0), ("zs", 2, 1, 1), ("zl", 2, 1, 1),
    ("zl", 1, 2, 0), ("xa", 3, 0), ("xa", 3, 1), ("zl", 1, 2, 1), ("zl", 3, 1, 0), ("zs", 3, 1, 0), ("zs", 3, 1, 1),
    ("zl", 3, 1, 1), ("zl", 2, 2, 0), ("z2s", 1, 0), ("z2l", 1, 0), ("fz", 0), ("zl", 2, 2, 1), ("xb", 2),
    ("x2a", 0), ("zb", 1), ("zl", 3, 2, 0), ("zl", 3, 2, 1), ("z2l", 1, 1), ("zb", 2), ("xb", 3), ("fx", 0),
    ("x2a", 1), ("z2s", 1, 1), ("zt", 2, 0), ("zt", 2, 2), ("zt", 2, 1), ("zb", 3), ("z2l", 1, 2), ("x2a", 2),
    ("zt", 3, 0), ("zt", 3, 2), ("fx", 1), ("zt", 3, 1), ("x2a", 3), ("fx", 2), ("fz", 1), ("fz", 2), ("fx", 3),
    ("fz", 3),
)
BF = jnp.bfloat16
F32 = jnp.float32


def mod(value, n):
    return lax.rem(value + 4 * n, n)


def kernel(
    limit, x_hbm, s_hbm, g_hbm, out_ref, *scratch
):
    x, z, yl, yh, c = (lax.axis_index(name) for name in AXES)
    quarter = NZ * 2 * HD
    xv, sv, xd, xs, gb, gt, ty, ry, nsrc, n1, n2, n3 = scratch[:12]
    (
        ld_sem, out_sem, rs_sem, g_own, g_rs, xo_rs, xp_rs, xf_rs,
        xl_rs, xb_rs, zl_rs, zs_rs, zf_rs, z2l_rs, z2s_rs, x2_rs, fz_rs, fx_rs,
        y_rs, n_rs,
    ) = scratch[12:32]
    (
        wx, wz, rxl, rxb, rzl, rzs, rzf, vz, vb, uz, ub, r2zl, r2zs, r2x, f2z, f2x,
    ) = (scratch[32 + k :: 16] for k in range(16))

    def push(src, dst, ss, rs, dev):
        pltpu.make_async_remote_copy(
            src_ref=src, dst_ref=dst, send_sem=ss, recv_sem=rs, device_id=dev, device_id_type=MESH
        ).start()

    def arrived(dst, rs):
        pltpu.make_async_remote_copy(
            src_ref=dst, dst_ref=dst, send_sem=rs, recv_sem=rs, device_id={"c": 1 - c}, device_id_type=MESH
        ).wait_recv()

    def sent(src, ss):
        pltpu.make_async_remote_copy(
            src_ref=src, dst_ref=src, send_sem=ss, recv_sem=ss, device_id={"c": 1 - c}, device_id_type=MESH
        ).wait_send()

    def order_x(i):
        if isinstance(i, int):
            return mod(x + (2, 1, 3, 0)[i], NX)
        return mod(x + jnp.where(i == 0, 2, jnp.where(i == 1, 1, jnp.where(i == 2, 3, 0))), NX)

    def load(i):
        xq = order_x(i)
        cols = pl.ds(pl.multiple_of(xq * quarter, quarter), quarter)
        return pltpu.make_async_copy(x_hbm.at[:, cols], xv.at[:, cols], ld_sem.at[i])

    load(0).start()
    own_g = pltpu.make_async_copy(g_hbm.at[pl.ds(pl.multiple_of(yh * 256, 256), 256), :], gb.at[0, 0], ld_sem.at[NX])
    scale_load = pltpu.make_async_copy(s_hbm, sv, ld_sem.at[NX + 1])
    scale_load.start()

    barrier = pltpu.get_barrier_semaphore()

    def greet(dev):
        pl.semaphore_signal(barrier, inc=1, device_id=dev, device_id_type=MESH)

    plane = [(k, e, w) for k in range(NX) for e in range(NC) for w in range(NZ) if (k, e, w) != (0, 0, 0)]
    y_line = [(a, b) for a in range(NH) for b in range(NL) if (a, b) != (0, 0)]

    def plane_dev(k, e, w):
        return {"x": mod(x + k, NX), "c": mod(c + e, NC), "z": mod(z + w, NZ)}

    def y_dev(a, b):
        return {"yh": mod(yh + a, NH), "yl": mod(yl + b, NL)}

    met = [(1, 0, 0), (NX - 1, 0, 0), (0, 1, 0), (0, 0, 1), (0, 0, NZ - 1)]
    for step in met:
        greet(plane_dev(*step))
    for a, b in y_line:
        greet(y_dev(a, b))

    for i in range(1, NX):
        load(i).start()
    own_g.start()

    def slab(k):
        return g_hbm.at[pl.ds(pl.multiple_of(mod(k, NH) * 256, 256), 256), :]

    beside = {"yl": 1 - yl}
    beyond = {"yh": mod(yh + 2 * yl - 1, NH), "yl": 1 - yl}

    def offset(p):
        if p % 2 == 0:
            return p
        return jnp.where(yl == 1, p, NH - p)

    def send_first_g():
        push(slab(yh), gb.at[0, 1], out_sem.at[1], g_rs.at[0], beside)
        push(slab(yh + 1 - 2 * yl), gb.at[0, 2], out_sem.at[1], g_rs.at[0], beside)

    def send_g(o):
        if o == 0:
            push(slab(yh), gb.at[1 + 2 * yl, 2], out_sem.at[1], g_rs.at[1 + 2 * yl], beyond)
        else:
            user = mod(yh - o, NH)
            push(slab(user), gb.at[o, 0], out_sem.at[1], g_own.at[o], {"yh": user})

    soon = 1 + 2 * yl
    late = 3 - 2 * yl

    def op_g(k):
        if k == 0:
            arrived(gb.at[soon, 0], g_own.at[soon])
            push(gb.at[soon, 0], gb.at[soon, 1], out_sem.at[1], g_rs.at[soon], beside)
        elif k == 1:
            arrived(gb.at[late, 0], g_own.at[late])
        elif k == 2:
            push(gb.at[soon, 0], gb.at[2, 2], out_sem.at[1], g_rs.at[2], beyond)
        elif k == 3:
            arrived(gb.at[2, 0], g_own.at[2])
            push(gb.at[2, 0], gb.at[2, 1], out_sem.at[1], g_rs.at[2], beside)
        else:
            push(gb.at[late, 0], gb.at[late, 1], out_sem.at[1], g_rs.at[late], beside)
            push(gb.at[2, 0], gb.at[3 - 2 * yl, 2], out_sem.at[1], g_rs.at[3 - 2 * yl], beyond)

    scale_load.wait()
    scales = sv[...].astype(F32).T.astype(BF)
    blocks = scales.shape[1]

    def dequant(b):
        pick = (lax.broadcasted_iota(jnp.int32, (blocks, HD), 0) == b).astype(F32).astype(BF)
        spread = jnp.dot(scales, pick, preferred_element_type=F32)
        v = xv[:, pl.ds(pl.multiple_of(b * HD, HD), HD)].astype(F32)
        return (v * spread).astype(BF)

    def prepare(i):
        xq = order_x(i)
        load(i).wait()

        @pl.loop(0, NZ, unroll=4)
        def _(zq):
            par, j = lax.rem(zq, 2), zq // 2
            s = lax.rem(zq + yl, 2)
            b = (xq * NZ + zq) * 2
            xs[xq * 8 + par * 4 + j] = dequant(b + 1 - s)
            xd[c, xq, par, j] = dequant(b + s)

    def share(i):
        xq = order_x(i)
        for par in range(2):
            s_out = lax.rem(par + yl + 1, 2)
            partner = {"yh": mod(yh + s_out * (2 * yl - 1), NH), "yl": 1 - yl}
            push(xs.at[pl.ds(xq * 8 + par * 4, 4)], xd.at[2 + c, xq, par], out_sem.at[0], xp_rs.at[xq, par], partner)

    def share_chip(i):
        xq = order_x(i)
        push(xd.at[c, xq], xd.at[c, xq], out_sem.at[0], xo_rs.at[xq], {"c": 1 - c})

    prepare(0)
    pl.semaphore_wait(barrier, len(met) + len(y_line))
    share(0)
    send_first_g()
    share_chip(0)

    @pl.loop(1, NX)
    def _(i):
        prepare(i)
        share(i)

    near = lax.rem(yl + 1, 2)

    def pass_on(i):
        xq = order_x(i)
        for k in range(2):
            par = lax.rem(near + k, 2)
            arrived(xd.at[2 + c, xq, par], xp_rs.at[xq, par])
            push(xd.at[2 + c, xq, par], xd.at[2 + c, xq, par], out_sem.at[0], xf_rs.at[xq], {"c": 1 - c})

    def product(p, i, xq):
        for par in range(2):
            s = lax.rem(par + yl, 2)
            lhs = jnp.concatenate([gt[0], gt[1 + s]], axis=1)
            for jj in range(2):
                rhs = jnp.concatenate(
                    [
                        jnp.concatenate([xd[k, xq, par, 2 * jj + e] for k in range(4)], axis=0)
                        for e in range(2)
                    ],
                    axis=1,
                )
                res = jnp.dot(lhs, rhs, preferred_element_type=F32).astype(BF)
                for e in range(2):
                    j = 2 * jj + e
                    wx[p][xq, par, j] = res[: ROWS[p], e * HD : (e + 1) * HD]
                    wz[p][2 * j + par, i] = res[ROWS[p] :, e * HD : (e + 1) * HD]

    def xdir(par):
        return 1 - 2 * par

    def after_product(p, i, xq):
        def when(k, run):
            if isinstance(i, int):
                if i == k:
                    run()
            else:
                pl.when(i == k)(run)

        def first():
            for par in range(2):
                d = xdir(par)
                push(wx[p].at[xq, par], rxl[p].at[par], rs_sem.at[p], xl_rs.at[p, par], {"x": mod(x + d, NX)})

        def second():
            push(wx[p].at[xq, 1], rxb[p].at[3], rs_sem.at[p], xb_rs.at[p], {"x": xq})

        def third():
            push(wx[p].at[xq, 0], rxb[p].at[2], rs_sem.at[p], xb_rs.at[p], {"x": xq})

        when(0, first)
        when(1, second)
        when(1, lambda: start_z(p, 0))
        when(2, third)
        when(3, lambda: start_z(p, 1))

    def start_z(p, h):
        z_long(p, 0, h)
        z_short(p, 0, h)

    def take_g(p):
        o = offset(p)
        if p == 0:
            own_g.wait()
        arrived(gb.at[o, pl.ds(1, 2)], g_rs.at[o])
        for k in range(3):
            gt[k] = gb[o, k].astype(F32).T.astype(BF)

    def op_m(p, i):
        if i == 0:
            pass_on(0)
            share_chip(1)
            take_g(0)
        xq = order_x(i)
        arrived(xd.at[1 - c, xq], xo_rs.at[xq])
        arrived(xd.at[3 - c, xq], xf_rs.at[xq])
        product(p, i, xq)
        after_product(p, i, xq)
        if i < NX - 1:
            pass_on(i + 1)
            if i < NX - 2:
                share_chip(i + 2)
        if i == 0:
            for o in (1, 3, 0):
                send_g(o)
        if i == 1:
            send_g(2)

    def op_n(p):
        take_g(p)

        @pl.loop(0, NX)
        def _(i):
            xq = order_x(i)
            product(p, i, xq)
            after_product(p, i, xq)

    def z_long(p, k, h):
        d = xdir(h)
        dst, rs = (rzf[p].at[h], zf_rs.at[p]) if k == 3 else (rzl[p].at[k, h], zl_rs.at[p, k, h])
        src = wz[p].at[mod(z + (4 - k) * d, NZ), pl.ds(2 * h, 2)]
        push(src, dst, rs_sem.at[p], rs, {"z": mod(z + d, NZ)})

    def z_short(p, k, h):
        d = xdir(h)
        dst, rs = (rzf[p].at[2 + h], zf_rs.at[p]) if k == 2 else (rzs[p].at[k, h], zs_rs.at[p, k, h])
        src = wz[p].at[mod(z - (3 - k) * d, NZ), pl.ds(2 * h, 2)]
        push(src, dst, rs_sem.at[p], rs, {"z": mod(z - d, NZ)})

    def z_long_add(p, k, h):
        t = mod(z + (3 - k) * xdir(h), NZ)
        arrived(rzl[p].at[k, h], zl_rs.at[p, k, h])
        for e in range(2):
            wz[p][t, 2 * h + e] = (wz[p][t, 2 * h + e].astype(F32) + rzl[p][k, h, e].astype(F32)).astype(BF)
        z_long(p, k + 1, h)

    def z_short_add(p, k, h):
        t = mod(z - (2 - k) * xdir(h), NZ)
        arrived(rzs[p].at[k, h], zs_rs.at[p, k, h])
        for e in range(2):
            wz[p][t, 2 * h + e] = (wz[p][t, 2 * h + e].astype(F32) + rzs[p][k, h, e].astype(F32)).astype(BF)
        z_short(p, k + 1, h)

    def pdir(p):
        return 1 - 2 * (p % 2)

    def z2_long(p, k, t):
        dst, rs = (f2z[p].at[0], fz_rs.at[p]) if k == 3 else (r2zl[p].at[k], z2l_rs.at[p, k])
        push(vb[p].at[t], dst, rs_sem.at[p], rs, {"z": mod(z + pdir(p), NZ)})

    def z2_short(p, k, t):
        dst, rs = (f2z[p].at[1], fz_rs.at[p]) if k == 2 else (r2zs[p].at[k], z2s_rs.at[p, k])
        push(vb[p].at[t], dst, rs_sem.at[p], rs, {"z": mod(z - pdir(p), NZ)})

    def z2_long_add(p, k):
        t = mod(z + (3 - k) * pdir(p), NZ)
        arrived(r2zl[p].at[k], z2l_rs.at[p, k])
        vb[p][t] = (vz[p][t] + r2zl[p][k].astype(F32)).astype(BF)
        z2_long(p, k + 1, t)

    def z2_short_add(p, k):
        t = mod(z - (2 - k) * pdir(p), NZ)
        arrived(r2zs[p].at[k], z2s_rs.at[p, k])
        vb[p][t] = (vz[p][t] + r2zs[p][k].astype(F32)).astype(BF)
        z2_short(p, k + 1, t)

    def op_xa(p, par):
        d = xdir(par)
        t = mod(x + d, NX)
        arrived(rxl[p].at[par], xl_rs.at[p, par])
        for j in range(4):
            wx[p][t, par, j] = (wx[p][t, par, j].astype(F32) + rxl[p][par, j].astype(F32)).astype(BF)
        push(wx[p].at[t, par], rxb[p].at[par], rs_sem.at[p], xb_rs.at[p], {"x": t})

    def op_xb(p):
        arrived(rxb[p], xb_rs.at[p])
        for par in range(2):
            for j in range(4):
                vz[p][2 * j + par] = (
                    wx[p][x, par, j].astype(F32) + rxb[p][2 + par, j].astype(F32) + rxb[p][par, j].astype(F32)
                )
        if p in TREE:
            start_tree(p)
            return
        d = pdir(p)
        t = mod(z + 4 * d, NZ)
        vb[p][t] = vz[p][t].astype(BF)
        z2_long(p, 0, t)
        t = mod(z - 3 * d, NZ)
        vb[p][t] = vz[p][t].astype(BF)
        z2_short(p, 0, t)

    def op_zb(p):
        arrived(rzf[p], zf_rs.at[p])
        for h in range(2):
            for e in range(2):
                uz[p][2 * h + e] = (
                    wz[p][z, 2 * h + e].astype(F32) + rzf[p][2 + h, e].astype(F32) + rzf[p][h, e].astype(F32)
                )
        d = pdir(p)
        ub[p][0] = uz[p][0].astype(BF)
        push(ub[p].at[0], r2x[p], rs_sem.at[p], x2_rs.at[p], {"x": mod(x + d, NX)})
        k = 2 - p % 2
        ub[p][k] = uz[p][k].astype(BF)
        push(ub[p].at[k], f2x[p].at[1], rs_sem.at[p], fx_rs.at[p], {"x": mod(x - d, NX)})

    def op_x2a(p):
        k = 1 + p % 2
        arrived(r2x[p], x2_rs.at[p])
        ub[p][k] = (uz[p][k] + r2x[p][...].astype(F32)).astype(BF)
        push(ub[p].at[k], f2x[p].at[0], rs_sem.at[p], fx_rs.at[p], {"x": mod(x + pdir(p), NX)})

    s_mine = lax.rem(z + yl, 2)
    stays = s_mine == yl

    def z_tree(p, k):
        d = pdir(p)
        if k == 0:
            t, got, rs, slot = mod(z + 3 * d, NZ), r2zl[p].at[0], z2l_rs.at[p, 0], 0
        elif k == 1:
            t, got, rs, slot = mod(z + d, NZ), r2zl[p].at[1], z2l_rs.at[p, 1], 1
        else:
            t, got, rs, slot = mod(z - 2 * d, NZ), r2zs[p].at[0], z2s_rs.at[p, 0], 2
        arrived(got, rs)
        vb[p][t] = (vz[p][t] + got[...].astype(F32)).astype(BF)
        push(vb[p].at[t], f2z[p].at[slot], rs_sem.at[p], fz_rs.at[p], {"z": t})

    def start_tree(p):
        d = pdir(p)
        near, back = {"z": mod(z + d, NZ)}, {"z": mod(z - d, NZ)}
        for steps, dst, rs, dev in (
            (4, r2zl[p].at[0], z2l_rs.at[p, 0], near),
            (-3, r2zs[p].at[0], z2s_rs.at[p, 0], back),
            (2, r2zl[p].at[1], z2l_rs.at[p, 1], near),
            (-1, f2z[p].at[3], fz_rs.at[p], back),
        ):
            t = mod(z + steps * d, NZ)
            vb[p][t] = vz[p][t].astype(BF)
            push(vb[p].at[t], dst, rs_sem.at[p], rs, dev)

    def give(p, first, rows):
        part = pl.ds(first, rows)
        far = 1 if p > 0 else 0

        def remote():
            o = offset(p)
            dev = {"yh": mod(yh + o, NH), "yl": s_mine}
            push(ty.at[p, part], ry.at[o, part], out_sem.at[2 + far], y_rs.at[far], dev)

        if p > 0:
            remote()
        else:
            pl.when(jnp.logical_not(stays))(remote)

            @pl.when(stays)
            def _():
                ry[0, part] = ty[0, part]

    def op_fx(p):
        arrived(f2x[p], fx_rs.at[p])
        ty[p, ROWS[p] :] = uz[p][3] + f2x[p][0].astype(F32) + f2x[p][1].astype(F32)
        give(p, ROWS[p], HD - ROWS[p])

    def op_fz(p):
        arrived(f2z[p], fz_rs.at[p])
        total = vz[p][z]
        for k in range(f2z[p].shape[0]):
            total += f2z[p][k].astype(F32)
        ty[p, : ROWS[p]] = total
        give(p, 0, ROWS[p])

    ops = {
        "G": op_g, "M": op_m, "N": op_n, "xa": op_xa, "xb": op_xb, "zl": z_long_add, "zs": z_short_add,
        "z2l": z2_long_add, "z2s": z2_short_add, "zb": op_zb, "x2a": op_x2a, "fx": op_fx, "fz": op_fz, "zt": z_tree,
    }

    for name, *where in SEQUENCE:
        ops[name](*where)

    sent(xd.at[pl.ds(0, 3)], out_sem.at[0])
    sent(xs.at[pl.ds(0, 22)], out_sem.at[1])
    for p in range(PHASES):
        sent(xs.at[pl.ds(0, 31)], rs_sem.at[p])
    arrived(ry.at[pl.ds(1, PHASES - 1)], y_rs.at[1])

    @pl.when(jnp.logical_not(stays))
    def _():
        arrived(ry.at[0], y_rs.at[0])

    total = ry[0] + ry[1] + ry[2] + ry[3]
    part = jnp.sum(total * total, axis=0, keepdims=True)

    def spot(k, e, w):
        return (mod(x + k, NX) * NC + mod(c + e, NC)) * NZ + mod(z + w, NZ)

    mine = spot(0, 0, 0)
    nsrc[0] = part
    for step in plane:
        push(nsrc.at[0], n1.at[mine], out_sem.at[4], n_rs.at[0], plane_dev(*step))
    n1[mine] = part
    out_ref[...] = total.T
    arrived(n1.at[pl.ds(0, len(plane))], n_rs.at[0])
    part = jnp.sum(n1[...], axis=0)

    def place(a, b):
        return mod(yh + a, NH) * NL + mod(yl + b, NL)

    nsrc[2] = part
    for a, b in y_line:
        push(nsrc.at[2], n3.at[place(0, 0)], out_sem.at[6], n_rs.at[2], y_dev(a, b))
    n3[place(0, 0)] = part
    sent(n1.at[pl.ds(0, len(plane))], out_sem.at[4])

    @pl.when(jnp.logical_not(stays))
    def _():
        sent(ty.at[0], out_sem.at[2])

    sent(ty.at[pl.ds(1, PHASES - 1)], out_sem.at[3])
    arrived(n3.at[pl.ds(0, len(y_line))], n_rs.at[2])
    part = jnp.sum(n3[...], axis=0)
    whole = jnp.sum(part, axis=1, keepdims=True)
    out_ref[...] = out_ref[...] * jnp.minimum(jnp.float32(1.0), jnp.float32(limit) / jnp.sqrt(whole))
    sent(n3.at[pl.ds(0, len(y_line))], out_sem.at[6])


def phase_scratch(rx, rz, last):
    shapes = [
        (NX, 2, 4, rx), (NZ, NX, rz), (2, 4, rx), (4, 4, rx), (3, 2, 2, rz), (2, 2, 2, rz), (4, 2, rz),
        (NZ, rx), (NZ, rx), (NX, rz), (NX, rz), (3, rx), (2, rx), (rz,), (last, rx), (2, rz),
    ]
    return [pltpu.VMEM((*s, HD), F32 if k in (7, 9) else BF) for k, s in enumerate(shapes)]


def body(stash_values, stash_scales, value_grad):
    tokens, width = stash_values.shape
    limit = math.sqrt(width * HD * lax.axis_size("yh") * lax.axis_size("c"))
    dma = pltpu.SemaphoreType.DMA
    return pl.pallas_call(
        functools.partial(kernel, limit),
        out_shape=jax.ShapeDtypeStruct((HD, HD), F32),
        in_specs=[
            pl.BlockSpec(memory_space=pl.ANY),
            pl.BlockSpec(memory_space=pl.ANY),
            pl.BlockSpec(memory_space=pl.ANY),
        ],
        out_specs=pl.BlockSpec(memory_space=pltpu.VMEM),
        scratch_shapes=[
            pltpu.VMEM((tokens, width), BF),
            pltpu.VMEM((stash_scales.shape[1], tokens), BF),
            pltpu.VMEM((4, NX, 2, 4, TOK, HD), BF),
            pltpu.VMEM((NX * 8, TOK, HD), BF),
            pltpu.VMEM((NH, 3, 2 * TOK, HD), BF),
            pltpu.VMEM((3, HD, 2 * TOK), BF),
            pltpu.VMEM((PHASES, HD, HD), F32),
            pltpu.VMEM((PHASES, HD, HD), F32),
            pltpu.VMEM((3, 1, HD), F32),
            pltpu.VMEM((NX * NC * NZ, 1, HD), F32),
            pltpu.VMEM((NZ, 1, HD), F32),
            pltpu.VMEM((NH * NL, 1, HD), F32),
            dma((NX + 2,)),
            dma((7,)),
            dma((PHASES,)),
            dma((NH,)),
            dma((NH,)),
            dma((NX,)),
            dma((NX, 2)),
            dma((NX,)),
            dma((PHASES, 2)),
            dma((PHASES,)),
            dma((PHASES, 3, 2)),
            dma((PHASES, 2, 2)),
            dma((PHASES,)),
            dma((PHASES, 3)),
            dma((PHASES, 2)),
            dma((PHASES,)),
            dma((PHASES,)),
            dma((PHASES,)),
            dma((2,)),
            dma((3,)),
            *(ref for p, rows in enumerate(ROWS) for ref in phase_scratch(rows, HD - rows, 4 if p in TREE else 2)),
        ],
        compiler_params=pltpu.CompilerParams(
            collective_id=0, has_side_effects=True, vmem_limit_bytes=56 * 1024 * 1024
        ),
    )(stash_values, stash_scales.T, value_grad)


def solution(mesh):
    torus = Mesh(mesh.devices.reshape(NX, NZ, NL, NH, NC), AXES)
    rows = ("x", "z", "yl", "yh", "c")
    return jax.shard_map(
        body,
        mesh=torus,
        in_specs=(P(rows, None), P(rows, None), P(("x", "z", "yl"), ("yh", "c"))),
        out_specs=P(("x", "z", "yl"), ("yh", "c")),
        check_vma=False,
    )
```
